256 devices in a mesh: term: 8 (over z), sector: 32 (over y, x, core).
Axes of the slice: x: 4, y: 4, z: 8, core: 2. Of those that a mesh axis runs over, the one named last changes fastest.
Arguments:
- left_ops: float32 [8, 32, 512, 512], P('term', 'sector'), may hold values from -1 to 2, as said below
- right_ops: float32 [8, 32, 512, 512], P('term', 'sector'), may hold values from -1 to 2, as said below
- hop_left: float32 [8, 32, 512, 512], P('term', 'sector'), may hold values from -0.0625 to 0.0625
- hop_right: float32 [8, 32, 512, 512], P('term', 'sector'), may hold values from -0.0625 to 0.0625
- v_left: bfloat16 [8, 32, 512, 128], P('term', 'sector'), may hold values from -0.5 to 0.5
- v_right: bfloat16 [8, 32, 128, 512], P('term', 'sector'), may hold values from -1.5 to 1.5
- zero_blocks: bfloat16 [32, 128, 128], P('sector'), may hold values from -6 to 6
- links: int32 [8, 32], P('term', 'sector'), may hold values from 0 to 31
- block_dims: int32 [32], P('sector'), may hold values from 128 to 512
Outputs:
- solution: float32 [32, 512, 512], P('sector')
- residual: float32 [32, 512, 512], P('sector')
The draws below stay inside these ranges and needn't reach their ends.
Inputs may be any that keep to these rules, and one draw needn't show every extreme that they name: Every block left_ops[t, s] and right_ops[t, s] is symmetric and positive definite. `right_ops`: every block is symmetric and positive definite.
All inputs are finite; a program needn't handle non-finite values.
Results may differ from the reference program's by a relative error of at most 0.0003.
Values may be sent and summed in bfloat16 or wider, within the bound.
No kernel may reach another device: no remote copies, remote signals or barrier semaphores. Data moves between devices by JAX's collectives and lax.ppermute only.
A program may use at most 64 MiB of HBM per device.

```python
import jax
import jax.numpy as jnp
from jax import lax

BLOCK = 512
ZBLOCK = 128
ITERS = 3
TERMS = 8
SECTORS = 32


def spd_blocks(key, salt):
    key = jax.random.fold_in(key, salt)
    key_noise, key_diag = jax.random.split(key)
    shape = (TERMS, SECTORS, BLOCK, BLOCK)
    noise = jax.random.normal(key_noise, shape, jnp.float32) * (0.12 / BLOCK ** 0.5)
    diag_vals = jnp.exp(jax.random.uniform(key_diag, shape[:3], jnp.float32, jnp.log(0.35), jnp.log(1.2)))
    noise = (noise + jnp.swapaxes(noise, -1, -2)) * 0.7071
    identity = jnp.eye(BLOCK, dtype=jnp.float32)
    return noise + diag_vals[..., None] * identity


def draw_left_ops(key, part):
    return spd_blocks(key, 11)


def draw_right_ops(key, part):
    return spd_blocks(key, 23)


def with_ends(entries, rng, smallest, high):
    longest = entries.shape.index(max(entries.shape))
    spots = []
    for shift in (0, 1):
        where = [jax.random.randint(jax.random.fold_in(rng, axis), (), 0, length) for axis, length in enumerate(entries.shape)]
        where[longest] = (where[longest] + shift) % entries.shape[longest]
        spots.append(tuple(where))
    return entries.at[spots[0]].set(smallest).at[spots[1]].set(high)


def block_scale(key, shape, shards, smallest, largest):
    factor_of, own = 1.0, jax.random.fold_in(key, 6)
    for axis_at, blocks in shards:
        draws = jnp.exp(jax.random.uniform(jax.random.fold_in(own, axis_at), (blocks,), jnp.float32, smallest / len(shards), largest / len(shards)))
        factor_of = factor_of * jnp.repeat(draws, shape[axis_at] // blocks).reshape([-1 if axis == axis_at else 1 for axis in range(len(shape))])
    return factor_of


def bell_draw(own_key, extent, spread, bound, shards=(), held_as=jnp.bfloat16):
    values = jax.random.normal(own_key, extent, jnp.float32) * spread
    if len(shards) > 0:
        values = block_scale(own_key, extent, shards, -0.22, 0.18) * values
    return jnp.clip(values, min=-bound, max=bound).astype(held_as)


def setup_inputs(seed: int = 0) -> dict:
    arg_keys = jax.random.split(jax.random.key(seed), 10)
    left_ops = draw_left_ops(jax.random.fold_in(arg_keys[9], 71), 0)
    right_ops = draw_right_ops(jax.random.fold_in(arg_keys[9], 71), 0)
    hop_left = bell_draw(arg_keys[2], (TERMS, SECTORS, BLOCK, BLOCK), (2 * BLOCK * TERMS) ** -0.5, 0.0625, ((0, 8), (1, 32)), jnp.float32)
    hop_right = bell_draw(arg_keys[3], (TERMS, SECTORS, BLOCK, BLOCK), (2 * BLOCK * TERMS) ** -0.5, 0.0625, ((0, 8), (1, 32)), jnp.float32)
    v_left = bell_draw(arg_keys[4], (TERMS, SECTORS, BLOCK, ZBLOCK), ZBLOCK ** -0.5, 0.5, ((0, 8), (1, 32)))
    v_right = bell_draw(arg_keys[5], (TERMS, SECTORS, ZBLOCK, BLOCK), 0.25, 1.5, ((0, 8), (1, 32)))
    zero_blocks = bell_draw(arg_keys[6], (SECTORS, ZBLOCK, ZBLOCK), 1.0, 6.0, ((0, 32),))
    links = with_ends(jax.random.randint(arg_keys[7], (TERMS, SECTORS), 0, SECTORS), jax.random.fold_in(arg_keys[7], 1), 0, SECTORS - 1).astype(jnp.int32)
    block_dims = with_ends(jax.random.randint(arg_keys[8], (SECTORS,), BLOCK // 4, BLOCK + 1), jax.random.fold_in(arg_keys[8], 1), BLOCK // 4, BLOCK).astype(jnp.int32)
    return dict(left_ops=left_ops, right_ops=right_ops, hop_left=hop_left, hop_right=hop_right, v_left=v_left, v_right=v_right, zero_blocks=zero_blocks, links=links, block_dims=block_dims)


level_gap = 2.5
exact = lax.Precision.HIGHEST


def build_mask(block_dims):
    positions = jnp.arange(BLOCK, dtype=jnp.int32)
    live = positions[None, :] < block_dims[:, None]
    return jnp.logical_and(live[:, :, None], live[:, None, :]).astype(jnp.float32)


def operate(vector, live_mask, left_ops, right_ops, hop_left, hop_right):
    blank = jnp.zeros_like(vector[:1])
    after = jnp.concatenate([vector[1:], blank], 0)
    before = jnp.concatenate([blank, vector[:-1]], 0)

    def one_term(running, operands):
        left_op, right_op, hop_in, hop_out = operands
        inner_part = jnp.einsum('sij,sjk->sik', left_op, vector, precision=exact)
        running = running + jnp.einsum('sik,skl->sil', inner_part, right_op, precision=exact)
        ahead = jnp.einsum('sij,sjk->sik', hop_in, after, precision=exact)
        running = running + jnp.einsum('sik,skl->sil', ahead, hop_out, precision=exact)
        hop_in_prev = jnp.concatenate([jnp.zeros_like(hop_in[:1]), hop_in[:-1]], 0)
        hop_out_prev = jnp.concatenate([jnp.zeros_like(hop_out[:1]), hop_out[:-1]], 0)
        behind = jnp.einsum('sji,sjk->sik', hop_in_prev, before, precision=exact)
        running = running + jnp.einsum('sik,slk->sil', behind, hop_out_prev, precision=exact)
        return running, None

    running, unused = lax.scan(one_term, jnp.zeros(vector.shape, jnp.float32),
                               (left_ops, right_ops, hop_left, hop_right))
    return live_mask * (level_gap * vector + running)


def reference(left_ops, right_ops, hop_left, hop_right, v_left, v_right, zero_blocks, links, block_dims):
    live_mask = build_mask(block_dims)
    picked = zero_blocks[links].astype(jnp.float32)
    middle = jnp.einsum('tsij,tsjk->tsik', v_left.astype(jnp.float32), picked, precision=exact)
    source = -live_mask * jnp.einsum('tsik,tskl->sil', middle, v_right.astype(jnp.float32), precision=exact)
    solution = jnp.zeros_like(source)
    residual = source
    direction = source
    norm_now = jnp.sum(residual * residual)
    for sweep_index in range(ITERS):
        image_vec = operate(direction, live_mask, left_ops, right_ops, hop_left, hop_right)
        step_size = norm_now / jnp.sum(direction * image_vec)
        solution = solution + step_size * direction
        residual = residual - step_size * image_vec
        norm_next = jnp.sum(residual * residual)
        direction = residual + (norm_next / norm_now) * direction
        norm_now = norm_next
    return solution, residual
```

```python
import jax
import jax.numpy as jnp
from jax import lax
from jax.experimental import pallas as pl
from jax.experimental.pallas import tpu as pltpu
from jax.sharding import Mesh
from jax.sharding import PartitionSpec as P

SECTOR = ("sector_0", "sector_1", "core")
GROUP = ("term", "core")

level_gap = 2.5
N = 512
LANES = 128
PEERS = 16
ROWS = N // PEERS
CHUNKS = N // LANES
BODY = ROWS * CHUNKS
MESSAGE = BODY + 16
HALF = ROWS // 2
STEPS = 8.0
FINE = 64.0
MIDDLE = 16384.0

f32, bf16, i16 = jnp.float32, jnp.bfloat16, jnp.int16


def shifted(value, axis, steps):
    count = lax.axis_size(axis)
    first, last = (max(0, -steps), min(count, count - steps))
    return lax.ppermute(value, axis, [(source, source + steps) for source in range(first, last)])


def two_parts(value):
    high = value.astype(bf16)
    return high, (value - high.astype(f32)).astype(bf16)


def product(a, b):
    return jnp.dot(a, b, preferred_element_type=f32)


def lane_groups(a, b, c, d):
    lane = lax.broadcasted_iota(jnp.int32, (HALF, LANES), 1)
    return jnp.where(lane < 32, a, jnp.where(lane < 64, b, jnp.where(lane < 96, c, d)))


def slopes_of(codes):
    size = jnp.exp2((jnp.abs(codes) - MIDDLE) * (1.0 / FINE))
    return jnp.where(codes == 0.0, 0.0, jnp.where(codes < 0.0, -size, size))


def encode(rows, guess):
    if guess is None:
        slope_code = jnp.zeros((ROWS, 1), f32)
        rest = rows
    else:
        over = jnp.sum(rows * guess, axis=1, keepdims=True)
        under = jnp.sum(guess * guess, axis=1, keepdims=True)
        slope = over / jnp.maximum(under, 1e-37)
        size = jnp.maximum(jnp.abs(slope), 1e-30)
        code = jnp.round(jnp.clip(jnp.log2(size) * FINE, -16000.0, 16000.0)) + MIDDLE
        code = jnp.minimum(code, 32000.0)
        slope_code = jnp.where(jnp.abs(slope) < 1e-30, 0.0, jnp.where(slope < 0.0, -code, code))
        rest = rows - slopes_of(slope_code) * guess
    largest = jnp.max(jnp.abs(rest), axis=1, keepdims=True)
    scale_code = jnp.ceil(jnp.log2(jnp.maximum(largest, 1e-34) * (1.0 / 32700.0)) * STEPS)
    coded = jnp.round(rest * jnp.exp2(scale_code * (-1.0 / STEPS)))
    coded = jnp.clip(coded, -32767.0, 32767.0).astype(jnp.int32).astype(i16)
    side = lane_groups(scale_code[:HALF], slope_code[:HALF], scale_code[HALF:], slope_code[HALF:])
    return coded, side.astype(jnp.int32).astype(i16)


def put(out, index, coded, side):
    for b in range(CHUNKS):
        out[index, b * ROWS : (b + 1) * ROWS, :] = coded[:, b * LANES : (b + 1) * LANES]
    out[index, BODY:, :] = side


def decode(message, index, guess):
    side = message[index, BODY:, :].astype(jnp.int32).astype(f32)
    scales = jnp.exp2(side * (1.0 / STEPS))
    scale = jnp.concatenate([scales[:, 0:1], scales[:, 64:65]], axis=0)
    parts = [message[index, b * ROWS : (b + 1) * ROWS, :].astype(jnp.int32).astype(f32) for b in range(CHUNKS)]
    rows = jnp.concatenate(parts, axis=1) * scale
    if guess is not None:
        slopes = slopes_of(side)
        slope = jnp.concatenate([slopes[:, 32:33], slopes[:, 96:97]], axis=0)
        rows = rows + slope * guess
    return rows


def rows_at(d):
    return pl.ds(pl.multiple_of(d * ROWS, ROWS), ROWS)


def live_rows(dims, d):
    at = lax.broadcasted_iota(jnp.int32, (ROWS, N), 0) + d * ROWS
    col = lax.broadcasted_iota(jnp.int32, (ROWS, N), 1)
    return jnp.logical_and(at < dims, col < dims)


def split_kernel(left, right, hop_in, hop_out, left2, right2, hop_in2, hop_out2, back):
    for source, target in ((left, left2), (right, right2), (hop_in, hop_in2), (hop_out, hop_out2)):
        high, low = two_parts(source[0, 0])
        target[0], target[1] = high, low
    for at, source in ((0, hop_in), (2, hop_out)):
        high, low = two_parts(source[0, 0].T)
        back[at], back[at + 1] = high, low


def source_kernel(numbers, v_left, v_right, picked, out, part):
    middle = product(v_left[0, 0], picked[0])
    high, low = two_parts(middle)
    last = (middle - high.astype(f32) - low.astype(f32)).astype(bf16)
    part[...] = product(high, v_right[0, 0]) + product(low, v_right[0, 0]) + product(last, v_right[0, 0])
    dims = numbers[0]

    def one(d, carry):
        rows = jnp.where(live_rows(dims, d), -part[rows_at(d), :], 0.0)
        put(out, d, *encode(rows, None))
        return carry

    lax.fori_loop(0, PEERS, one, 0)


def sum_kernel(numbers, messages, first, second, out, *, bare):
    for c, mine in ((0, first), (1, second)):
        guess = None if bare else mine[0]
        total = jnp.zeros((ROWS, N), f32) if bare else level_gap * guess
        for t in range(PEERS // 2):
            total = total + decode(messages, 2 * t + c, guess)
        coded, side = encode(total, guess)
        for t in range(PEERS // 2):
            put(out, 2 * t + c, coded, side)


def dots_kernel(message, mine, out):
    def one(d, carry):
        rr, rw = carry
        r = mine[0, rows_at(d), :]
        w = decode(message, d, r)
        return rr + r * r, rw + r * w

    zero = jnp.zeros((ROWS, N), f32)
    rr, rw = lax.fori_loop(0, PEERS, one, (zero, zero))
    row = lax.broadcasted_iota(jnp.int32, (8, LANES), 0)
    tile = jnp.where(row == 0, jnp.sum(rr), jnp.where(row == 1, jnp.sum(rw), 0.0))
    out[...] = jnp.broadcast_to(tile[None], out.shape)


def steps_of(totals, past, first):
    total = jnp.sum(totals[...], axis=0)
    norm, along = total[0:1], total[1:2]
    if first:
        ratio = jnp.zeros_like(norm)
        step = norm / along
        back = ratio
    else:
        ratio = norm / past[0:1]
        step = norm / (along - ratio * norm / past[1:2])
        back = step * ratio / past[1:2]
    wide = lambda a: jnp.broadcast_to(a[:, 0:1], (ROWS, N))
    return norm, ratio, step, wide(step), wide(back)


def apply_kernel(numbers, own, after, before, *rest, count):
    if count == 0:
        (left, right, hop_in, hop_out, back_ops, r_out, out, halves, mids, image) = rest
    elif count == 1:
        (r_now, totals, left, right, hop_in, hop_out, back_ops, r_out, out, past_out, halves, mids, image) = rest
    else:
        (r_now, totals, r_old, past, left, right, hop_in, hop_out, back_ops, r_out, out, past_out, halves, mids, image) = rest
    if count > 0:
        was = None if count == 1 else past[...]
        norm, ratio, step, wide_step, wide_back = steps_of(totals, was, count == 1)
        row = lax.broadcasted_iota(jnp.int32, (8, LANES), 0)
        tile = jnp.where(row == 0, norm, jnp.where(row == 1, step, 0.0))
        if count == 1:
            tile = jnp.where(row == 2, step, tile)
        else:
            tile = jnp.where(row == 2, was[2:3], jnp.where(row == 3, step, jnp.where(row == 4, ratio, tile)))
        past_out[...] = tile
    for j, message in ((0, before), (1, own), (2, after)):

        def one(d, carry, j=j, message=message):
            at = rows_at(d)
            if count == 0:
                r = decode(message, d, None)
            else:
                r = r_now[j, at, :]
                w = decode(message, d, r)
                new = r - wide_step * w
                if count > 1:
                    new = new - wide_back * (r_old[j, at, :] - r)
                r = new
            r_out[j, at, :] = r
            high, low = two_parts(r)
            halves[j, 0, at, :] = high
            halves[j, 1, at, :] = low
            return carry

        lax.fori_loop(0, PEERS, one, 0)
    pairs = (
        (1, left[0], left[1], right[0], right[1]),
        (2, hop_in[0], hop_in[1], hop_out[0], hop_out[1]),
        (0, back_ops[0], back_ops[1], back_ops[2], back_ops[3]),
    )
    for k, (j, a_high, a_low, b_high, b_low) in enumerate(pairs):
        v_high, v_low = halves[j, 0], halves[j, 1]
        middle = product(a_high, v_high) + (product(a_high, v_low) + product(a_low, v_high))
        m_high, m_low = two_parts(middle)
        mids[0], mids[1] = m_high, m_low
        add = product(mids[0], b_high) + (product(mids[0], b_low) + product(mids[1], b_high))
        image[...] = add if k == 0 else image[...] + add
    dims = numbers[0]

    def send(d, carry):
        at = rows_at(d)
        rows = jnp.where(live_rows(dims, d), image[at, :], 0.0)
        put(out, d, *encode(rows, r_out[1, at, :]))
        return carry

    lax.fori_loop(0, PEERS, send, 0)


def last_kernel(own, r0, r1, r2, totals, past, solution, residual):
    was = past[...]
    norm, ratio, step, wide_step, wide_back = steps_of(totals, was, False)
    step0, step1, ratio1 = was[2:3], was[3:4], was[4:5]
    wide = lambda a: jnp.broadcast_to(a[:, 0:1], (ROWS, N))
    on2 = wide_step
    on1 = wide(step1 + step * ratio)
    on0 = wide(step0 + (step1 + step * ratio) * ratio1)

    def one(d, carry):
        at = rows_at(d)
        a, b, c = r0[0, at, :], r1[0, at, :], r2[0, at, :]
        w = decode(own, d, c)
        solution[0, at, :] = on0 * a + on1 * b + on2 * c
        residual[0, at, :] = c - wide_step * w - wide_back * (b - c)
        return carry

    lax.fori_loop(0, PEERS, one, 0)


smem = pl.BlockSpec(memory_space=pltpu.SMEM)
vmem = pl.BlockSpec(memory_space=pltpu.VMEM)
params = pltpu.CompilerParams(vmem_limit_bytes=60 * 2**20)
message_shape = jax.ShapeDtypeStruct((PEERS, MESSAGE, LANES), i16)
field3 = jax.ShapeDtypeStruct((3, N, N), f32)
small = jax.ShapeDtypeStruct((8, LANES), f32)
whole = jax.ShapeDtypeStruct((1, N, N), f32)


def block(shape, index):
    return pl.BlockSpec(shape, index)


def middle_block():
    return block((1, N, N), lambda i: (1, 0, 0))


def exchange(messages):
    return lax.all_to_all(messages, GROUP, 0, 0, tiled=True)


def body(left_ops, right_ops, hop_left, hop_right, v_left, v_right, zero_blocks, links, block_dims):
    core = lax.axis_index("core")
    place = lax.axis_index("term") * 2 + core
    pair = jax.ShapeDtypeStruct((2, N, N), bf16)
    four = jax.ShapeDtypeStruct((4, N, N), bf16)
    count = lax.axis_size(SECTOR)
    everyone = lax.all_to_all(jnp.broadcast_to(zero_blocks, (count, 128, 128)), SECTOR, 0, 0, tiled=True)
    left, right, hop_in, hop_out, back = pl.pallas_call(
        split_kernel, out_shape=(pair, pair, pair, pair, four), in_specs=[vmem] * 4, out_specs=(vmem,) * 5,
        compiler_params=params, name="split",
    )(left_ops, right_ops, hop_left, hop_right)
    back = shifted(back, SECTOR, 1)
    numbers = jnp.stack([block_dims[0], links[0, 0], place, core]).astype(jnp.int32)

    fixed = lambda rank: (lambda i, n: (0,) * rank)
    messages = pl.pallas_call(
        source_kernel, out_shape=message_shape,
        grid_spec=pltpu.PrefetchScalarGridSpec(
            num_scalar_prefetch=1, grid=(1,),
            in_specs=[
                block((1, 1, N, 128), fixed(4)), block((1, 1, 128, N), fixed(4)),
                block((1, 128, 128), lambda i, n: (n[1], 0, 0)),
            ],
            out_specs=block((PEERS, MESSAGE, LANES), fixed(3)),
            scratch_shapes=[pltpu.VMEM((N, N), f32)],
        ),
        compiler_params=params, name="source",
    )(numbers, v_left, v_right, everyone)

    def summed(messages, fields):
        bare = fields is None
        given = (jnp.zeros((2, ROWS, N), f32),) * 2 if bare else (fields,) * 2
        if bare:
            specs = [block((1, ROWS, N), lambda i, n: (0, 0, 0))] * 2
        else:
            specs = [block((1, ROWS, N), lambda i, n, c=c: (1 + c - n[3], n[2], 0)) for c in (0, 1)]
        return pl.pallas_call(
            lambda *refs: sum_kernel(*refs, bare=bare), out_shape=message_shape,
            grid_spec=pltpu.PrefetchScalarGridSpec(
                num_scalar_prefetch=1, grid=(1,),
                in_specs=[block((PEERS, MESSAGE, LANES), fixed(3))] + specs,
                out_specs=block((PEERS, MESSAGE, LANES), fixed(3)),
            ),
            compiler_params=params, name="sum",
        )(numbers, messages, *given)

    def dots(message, fields):
        return pl.pallas_call(
            dots_kernel, out_shape=jax.ShapeDtypeStruct((count, 8, LANES), f32), grid=(1,),
            in_specs=[block((PEERS, MESSAGE, LANES), lambda i: (0, 0, 0)), middle_block()],
            out_specs=block((count, 8, LANES), lambda i: (0, 0, 0)),
            compiler_params=params, name="dots",
        )(message, fields)

    def applied(step, own, after, before, extra):
        shapes = (field3, message_shape) + ((small,) if step else ())
        return pl.pallas_call(
            lambda *refs: apply_kernel(*refs, count=step), out_shape=shapes,
            in_specs=[smem] + [vmem] * (3 + len(extra) + 5), out_specs=(vmem,) * len(shapes),
            scratch_shapes=[pltpu.VMEM((3, 2, N, N), bf16), pltpu.VMEM((2, N, N), bf16), pltpu.VMEM((N, N), f32)],
            compiler_params=params, name="apply",
        )(numbers, own, after, before, *extra, left, right, hop_in, hop_out, back)

    own = exchange(summed(exchange(messages), None))
    fields, past = [], None
    for step in range(3):
        after, before = shifted(own, SECTOR, -1), shifted(own, SECTOR, 1)
        if step == 0:
            extra = ()
        else:
            totals = lax.all_to_all(dots(own, fields[-1]), SECTOR, 0, 0, tiled=True)
            extra = (fields[-1], totals) + (() if step == 1 else (fields[-2], past))
        now, messages, *tail = applied(step, own, after, before, extra)
        fields.append(now)
        past = tail[0] if tail else None
        own = exchange(summed(exchange(messages), now))
    totals = lax.all_to_all(dots(own, fields[-1]), SECTOR, 0, 0, tiled=True)
    return tuple(
        pl.pallas_call(
            last_kernel, out_shape=(whole, whole), grid=(1,),
            in_specs=[block((PEERS, MESSAGE, LANES), lambda i: (0, 0, 0))] + [middle_block()] * 3
            + [block((count, 8, LANES), lambda i: (0, 0, 0)), block((8, LANES), lambda i: (0, 0))],
            out_specs=(block((1, N, N), lambda i: (0, 0, 0)),) * 2,
            compiler_params=params, name="last",
        )(own, *fields, totals, past)
    )


def solution(mesh):
    finer = Mesh(mesh.devices.reshape(mesh.shape["term"], 4, 4, 2), ("term", "sector_0", "sector_1", "core"))
    both = P("term", SECTOR, None, None)
    in_specs = (both,) * 6 + (P(SECTOR, None, None), P("term", SECTOR), P(SECTOR))
    out_specs = (P(SECTOR, None, None), P(SECTOR, None, None))
    return jax.shard_map(body, mesh=finer, in_specs=in_specs, out_specs=out_specs, check_vma=False)
```

```python
import jax
import jax.numpy as jnp
from jax import lax
from jax.experimental import pallas as pl
from jax.experimental.pallas import tpu as pltpu
from jax.sharding import Mesh
from jax.sharding import PartitionSpec as P

SECTOR = ("sector_0", "sector_1", "core")
GROUP = ("term", "core")

level_gap = 2.5
N = 512
LANES = 128
PEERS = 16
ROWS = N // PEERS
CHUNKS = N // LANES
BODY = ROWS * CHUNKS
MESSAGE = BODY + 16
HALF = ROWS // 2
STEPS = 8.0
FINE = 64.0
MIDDLE = 16384.0

f32, bf16, i16 = jnp.float32, jnp.bfloat16, jnp.int16


def shifted(value, axis, steps):
    count = lax.axis_size(axis)
    first, last = (max(0, -steps), min(count, count - steps))
    return lax.ppermute(value, axis, [(source, source + steps) for source in range(first, last)])


def two_parts(value):
    high = value.astype(bf16)
    return high, (value - high.astype(f32)).astype(bf16)


def product(a, b):
    return jnp.dot(a, b, preferred_element_type=f32)


def lane_groups(a, b, c, d):
    lane = lax.broadcasted_iota(jnp.int32, (HALF, LANES), 1)
    return jnp.where(lane < 32, a, jnp.where(lane < 64, b, jnp.where(lane < 96, c, d)))


def slopes_of(codes):
    size = jnp.exp2((jnp.abs(codes) - MIDDLE) * (1.0 / FINE))
    return jnp.where(codes == 0.0, 0.0, jnp.where(codes < 0.0, -size, size))


def encode(rows, guess):
    if guess is None:
        slope_code = jnp.zeros((ROWS, 1), f32)
        rest = rows
    else:
        over = jnp.sum(rows * guess, axis=1, keepdims=True)
        under = jnp.sum(guess * guess, axis=1, keepdims=True)
        slope = over / jnp.maximum(under, 1e-37)
        size = jnp.maximum(jnp.abs(slope), 1e-30)
        code = jnp.round(jnp.clip(jnp.log2(size) * FINE, -16000.0, 16000.0)) + MIDDLE
        code = jnp.minimum(code, 32000.0)
        slope_code = jnp.where(jnp.abs(slope) < 1e-30, 0.0, jnp.where(slope < 0.0, -code, code))
        rest = rows - slopes_of(slope_code) * guess
    largest = jnp.max(jnp.abs(rest), axis=1, keepdims=True)
    scale_code = jnp.ceil(jnp.log2(jnp.maximum(largest, 1e-34) * (1.0 / 32700.0)) * STEPS)
    coded = jnp.round(rest * jnp.exp2(scale_code * (-1.0 / STEPS)))
    coded = jnp.clip(coded, -32767.0, 32767.0).astype(jnp.int32).astype(i16)
    side = lane_groups(scale_code[:HALF], slope_code[:HALF], scale_code[HALF:], slope_code[HALF:])
    return coded, side.astype(jnp.int32).astype(i16)


def put(out, index, coded, side):
    for b in range(CHUNKS):
        out[index, b * ROWS : (b + 1) * ROWS, :] = coded[:, b * LANES : (b + 1) * LANES]
    out[index, BODY:, :] = side


def decode(message, index, guess):
    side = message[index, BODY:, :].astype(jnp.int32).astype(f32)
    scales = jnp.exp2(side * (1.0 / STEPS))
    scale = jnp.concatenate([scales[:, 0:1], scales[:, 64:65]], axis=0)
    parts = [message[index, b * ROWS : (b + 1) * ROWS, :].astype(jnp.int32).astype(f32) for b in range(CHUNKS)]
    rows = jnp.concatenate(parts, axis=1) * scale
    if guess is not None:
        slopes = slopes_of(side)
        slope = jnp.concatenate([slopes[:, 32:33], slopes[:, 96:97]], axis=0)
        rows = rows + slope * guess
    return rows


def rows_at(d):
    return pl.ds(pl.multiple_of(d * ROWS, ROWS), ROWS)


def live_rows(dims, d):
    at = lax.broadcasted_iota(jnp.int32, (ROWS, N), 0) + d * ROWS
    col = lax.broadcasted_iota(jnp.int32, (ROWS, N), 1)
    return jnp.logical_and(at < dims, col < dims)


def split_kernel(left, right, hop_in, hop_out, left2, right2, hop_in2, hop_out2, back):
    for source, target in ((left, left2), (right, right2), (hop_in, hop_in2), (hop_out, hop_out2)):
        high, low = two_parts(source[0, 0])
        target[0], target[1] = high, low
    for at, source in ((0, hop_in), (2, hop_out)):
        high, low = two_parts(source[0, 0].T)
        back[at], back[at + 1] = high, low


def source_kernel(numbers, v_left, v_right, picked, out, part):
    middle = product(v_left[0, 0], picked[0])
    high, low = two_parts(middle)
    last = (middle - high.astype(f32) - low.astype(f32)).astype(bf16)
    part[...] = product(high, v_right[0, 0]) + product(low, v_right[0, 0]) + product(last, v_right[0, 0])
    dims = numbers[0]

    def one(d, carry):
        rows = jnp.where(live_rows(dims, d), -part[rows_at(d), :], 0.0)
        put(out, d, *encode(rows, None))
        return carry

    lax.fori_loop(0, PEERS, one, 0, unroll=4)


def sum_kernel(numbers, messages, first, second, out, *, bare):
    for c, mine in ((0, first), (1, second)):
        guess = None if bare else mine[0]
        total = jnp.zeros((ROWS, N), f32) if bare else level_gap * guess
        for t in range(PEERS // 2):
            total = total + decode(messages, 2 * t + c, guess)
        put(out, c, *encode(total, guess))


def dots_kernel(numbers, messages, mine, out, own):
    core = numbers[3]

    def one(d, carry):
        rr, rw = carry
        r = mine[0, rows_at(d), :]
        w = decode(messages, 2 * d + core, r)
        own[d] = messages[2 * d + core]
        return rr + r * r, rw + r * w

    zero = jnp.zeros((ROWS, N), f32)
    rr, rw = lax.fori_loop(0, PEERS, one, (zero, zero), unroll=4)
    row = lax.broadcasted_iota(jnp.int32, (8, LANES), 0)
    tile = jnp.where(row == 0, jnp.sum(rr), jnp.where(row == 1, jnp.sum(rw), 0.0))
    out[...] = jnp.broadcast_to(tile[None], out.shape)


def steps_of(totals, past, first):
    total = jnp.sum(totals[...], axis=0)
    norm, along = total[0:1], total[1:2]
    if first:
        ratio = jnp.zeros_like(norm)
        step = norm / along
        back = ratio
    else:
        ratio = norm / past[0:1]
        step = norm / (along - ratio * norm / past[1:2])
        back = step * ratio / past[1:2]
    wide = lambda a: jnp.broadcast_to(a[:, 0:1], (ROWS, N))
    return norm, ratio, step, wide(step), wide(back)


def apply_kernel(numbers, messages, far, *rest, count):
    if count == 0:
        (left, right, hop_in, hop_out, back_ops, r_out, out, halves, mids, image) = rest
    elif count == 1:
        (r_now, totals, left, right, hop_in, hop_out, back_ops, r_out, out, past_out, halves, mids, image) = rest
    else:
        (r_now, totals, r_old, past, left, right, hop_in, hop_out, back_ops, r_out, out, past_out, halves, mids, image) = rest
    if count > 0:
        was = None if count == 1 else past[...]
        norm, ratio, step, wide_step, wide_back = steps_of(totals, was, count == 1)
        row = lax.broadcasted_iota(jnp.int32, (8, LANES), 0)
        tile = jnp.where(row == 0, norm, jnp.where(row == 1, step, 0.0))
        if count == 1:
            tile = jnp.where(row == 2, step, tile)
        else:
            tile = jnp.where(row == 2, was[2:3], jnp.where(row == 3, step, jnp.where(row == 4, ratio, tile)))
        past_out[...] = tile
    core = numbers[3]
    for j, message, stride, first in ((1, messages, 2, core), (2 - 2 * core, messages, 2, 1 - core), (2 * core, far, 1, 0)):

        def one(d, carry, j=j, message=message, stride=stride, first=first):
            at = rows_at(d)
            if count == 0:
                r = decode(message, stride * d + first, None)
            else:
                r = r_now[j, at, :]
                w = decode(message, stride * d + first, r)
                new = r - wide_step * w
                if count > 1:
                    new = new - wide_back * (r_old[j, at, :] - r)
                r = new
            r_out[j, at, :] = r
            high, low = two_parts(r)
            halves[j, 0, at, :] = high
            halves[j, 1, at, :] = low
            return carry

        lax.fori_loop(0, PEERS, one, 0, unroll=4)
    pairs = (
        (1, left[0], left[1], right[0], right[1]),
        (2, hop_in[0], hop_in[1], hop_out[0], hop_out[1]),
        (0, back_ops[0], back_ops[1], back_ops[2], back_ops[3]),
    )
    for k, (j, a_high, a_low, b_high, b_low) in enumerate(pairs):
        v_high, v_low = halves[j, 0], halves[j, 1]
        middle = product(a_high, v_high) + (product(a_high, v_low) + product(a_low, v_high))
        m_high, m_low = two_parts(middle)
        mids[0], mids[1] = m_high, m_low
        add = product(mids[0], b_high) + (product(mids[0], b_low) + product(mids[1], b_high))
        image[...] = add if k == 0 else image[...] + add
    dims = numbers[0]

    def send(d, carry):
        at = rows_at(d)
        rows = jnp.where(live_rows(dims, d), image[at, :], 0.0)
        put(out, d, *encode(rows, r_out[1, at, :]))
        return carry

    lax.fori_loop(0, PEERS, send, 0, unroll=4)


def last_kernel(numbers, messages, r0, r1, r2, totals, past, solution, residual):
    core = numbers[3]
    was = past[...]
    norm, ratio, step, wide_step, wide_back = steps_of(totals, was, False)
    step0, step1, ratio1 = was[2:3], was[3:4], was[4:5]
    wide = lambda a: jnp.broadcast_to(a[:, 0:1], (ROWS, N))
    on2 = wide_step
    on1 = wide(step1 + step * ratio)
    on0 = wide(step0 + (step1 + step * ratio) * ratio1)

    def one(d, carry):
        at = rows_at(d)
        a, b, c = r0[0, at, :], r1[0, at, :], r2[0, at, :]
        w = decode(messages, 2 * d + core, c)
        solution[0, at, :] = on0 * a + on1 * b + on2 * c
        residual[0, at, :] = c - wide_step * w - wide_back * (b - c)
        return carry

    lax.fori_loop(0, PEERS, one, 0, unroll=4)


smem = pl.BlockSpec(memory_space=pltpu.SMEM)
vmem = pl.BlockSpec(memory_space=pltpu.VMEM)
params = pltpu.CompilerParams(vmem_limit_bytes=24 * 2**20)
message_shape = jax.ShapeDtypeStruct((PEERS, MESSAGE, LANES), i16)
spread_shape = jax.ShapeDtypeStruct((2, MESSAGE, LANES), i16)
field3 = jax.ShapeDtypeStruct((3, N, N), f32)
small = jax.ShapeDtypeStruct((8, LANES), f32)
whole = jax.ShapeDtypeStruct((1, N, N), f32)


def block(shape, index):
    return pl.BlockSpec(shape, index)


def exchange(messages):
    return lax.all_to_all(messages, GROUP, 0, 0, tiled=True)


def body(left_ops, right_ops, hop_left, hop_right, v_left, v_right, zero_blocks, links, block_dims):
    core = lax.axis_index("core")
    place = lax.axis_index("term") * 2 + core
    pair = jax.ShapeDtypeStruct((2, N, N), bf16)
    four = jax.ShapeDtypeStruct((4, N, N), bf16)
    count = lax.axis_size(SECTOR)
    everyone = lax.all_to_all(jnp.broadcast_to(zero_blocks, (count, 128, 128)), SECTOR, 0, 0, tiled=True)
    left, right, hop_in, hop_out, back = pl.pallas_call(
        split_kernel, out_shape=(pair, pair, pair, pair, four), in_specs=[vmem] * 4, out_specs=(vmem,) * 5,
        compiler_params=params, name="split",
    )(left_ops, right_ops, hop_left, hop_right)
    v_left, back = lax.optimization_barrier((v_left, back))
    back = shifted(back, SECTOR, 1)
    numbers = jnp.stack([block_dims[0], links[0, 0], place, core]).astype(jnp.int32)

    fixed = lambda rank: (lambda i, n: (0,) * rank)
    messages = pl.pallas_call(
        source_kernel, out_shape=message_shape,
        grid_spec=pltpu.PrefetchScalarGridSpec(
            num_scalar_prefetch=1, grid=(1,),
            in_specs=[
                block((1, 1, N, 128), fixed(4)), block((1, 1, 128, N), fixed(4)),
                block((1, 128, 128), lambda i, n: (n[1], 0, 0)),
            ],
            out_specs=block((PEERS, MESSAGE, LANES), fixed(3)),
            scratch_shapes=[pltpu.VMEM((N, N), f32)],
        ),
        compiler_params=params, name="source",
    )(numbers, v_left, v_right, everyone)

    def summed(messages, fields):
        bare = fields is None
        given = (jnp.zeros((2, ROWS, N), f32),) * 2 if bare else (fields,) * 2
        if bare:
            specs = [block((1, ROWS, N), lambda i, n: (0, 0, 0))] * 2
        else:
            specs = [block((1, ROWS, N), lambda i, n, c=c: (1 + c - n[3], n[2], 0)) for c in (0, 1)]
        return pl.pallas_call(
            lambda *refs: sum_kernel(*refs, bare=bare), out_shape=spread_shape,
            grid_spec=pltpu.PrefetchScalarGridSpec(
                num_scalar_prefetch=1, grid=(1,),
                in_specs=[block((PEERS, MESSAGE, LANES), fixed(3))] + specs,
                out_specs=block((2, MESSAGE, LANES), fixed(3)),
            ),
            compiler_params=params, name="sum",
        )(numbers, messages, *given)

    def dots(messages, fields):
        return pl.pallas_call(
            dots_kernel, out_shape=(jax.ShapeDtypeStruct((count, 8, LANES), f32), message_shape),
            grid_spec=pltpu.PrefetchScalarGridSpec(
                num_scalar_prefetch=1, grid=(1,),
                in_specs=[block((2 * PEERS, MESSAGE, LANES), fixed(3)), block((1, N, N), lambda i, n: (1, 0, 0))],
                out_specs=(block((count, 8, LANES), fixed(3)), block((PEERS, MESSAGE, LANES), fixed(3))),
            ),
            compiler_params=params, name="dots",
        )(numbers, messages, fields)

    def applied(step, messages, far, extra):
        shapes = (field3, message_shape) + ((small,) if step else ())
        return pl.pallas_call(
            lambda *refs: apply_kernel(*refs, count=step), out_shape=shapes,
            in_specs=[smem] + [vmem] * (2 + len(extra) + 5), out_specs=(vmem,) * len(shapes),
            scratch_shapes=[pltpu.VMEM((3, 2, N, N), bf16), pltpu.VMEM((2, N, N), bf16), pltpu.VMEM((N, N), f32)],
            compiler_params=params, name="apply",
        )(numbers, messages, far, *extra, left, right, hop_in, hop_out, back)

    def spread(rows):
        return lax.all_gather(rows, GROUP, axis=0, tiled=True)

    def across(own):
        pairs = [(i, i + 1) for i in range(1, count - 1, 2)]
        return lax.ppermute(own, SECTOR, pairs + [(b, a) for a, b in pairs])

    messages = spread(summed(exchange(messages), None))
    fields, past = [], None
    for step in range(3):
        if step == 0:
            own, extra = lax.dynamic_index_in_dim(messages.reshape(PEERS, 2, MESSAGE, LANES), core, 1, keepdims=False), ()
        else:
            partial, own = dots(messages, fields[-1])
            totals = lax.all_to_all(partial, SECTOR, 0, 0, tiled=True)
            extra = (fields[-1], totals) + (() if step == 1 else (fields[-2], past))
        now, rows, *tail = applied(step, messages, across(own), extra)
        fields.append(now)
        past = tail[0] if tail else None
        messages = spread(summed(exchange(rows), now))
    totals = lax.all_to_all(dots(messages, fields[-1])[0], SECTOR, 0, 0, tiled=True)
    return tuple(
        pl.pallas_call(
            last_kernel, out_shape=(whole, whole),
            grid_spec=pltpu.PrefetchScalarGridSpec(
                num_scalar_prefetch=1, grid=(1,),
                in_specs=[block((2 * PEERS, MESSAGE, LANES), fixed(3))] + [block((1, N, N), lambda i, n: (1, 0, 0))] * 3
                + [block((count, 8, LANES), fixed(3)), block((8, LANES), fixed(2))],
                out_specs=(block((1, N, N), fixed(3)),) * 2,
            ),
            compiler_params=params, name="last",
        )(numbers, messages, *fields, totals, past)
    )


def solution(mesh):
    finer = Mesh(mesh.devices.reshape(mesh.shape["term"], 4, 4, 2), ("term", "sector_0", "sector_1", "core"))
    both = P("term", SECTOR, None, None)
    in_specs = (both,) * 6 + (P(SECTOR, None, None), P("term", SECTOR), P(SECTOR))
    out_specs = (P(SECTOR, None, None), P(SECTOR, None, None))
    return jax.shard_map(body, mesh=finer, in_specs=in_specs, out_specs=out_specs, check_vma=False)
```

```python
import jax
import jax.numpy as jnp
from jax import lax
from jax.experimental import pallas as pl
from jax.experimental.pallas import tpu as pltpu
from jax.sharding import Mesh
from jax.sharding import PartitionSpec as P

SECTOR = ("sector_0", "sector_1", "core")
GROUP = ("term", "core")

level_gap = 2.5
N = 512
LANES = 128
PEERS = 16
ROWS = N // PEERS
CHUNKS = N // LANES
BODY = ROWS * CHUNKS
MESSAGE = BODY + 16
PACK = 2 * N + 32
HALF = ROWS // 2
STEPS = 8.0
FINE = 64.0
MIDDLE = 16384.0

f32, bf16, i16 = jnp.float32, jnp.bfloat16, jnp.int16


def shifted(value, axis, steps):
    count = lax.axis_size(axis)
    first, last = (max(0, -steps), min(count, count - steps))
    return lax.ppermute(value, axis, [(source, source + steps) for source in range(first, last)])


def two_parts(value):
    high = value.astype(bf16)
    return high, (value - high.astype(f32)).astype(bf16)


def product(a, b):
    return jnp.dot(a, b, preferred_element_type=f32)


def lane_groups(a, b, c, d):
    lane = lax.broadcasted_iota(jnp.int32, (HALF, LANES), 1)
    return jnp.where(lane < 32, a, jnp.where(lane < 64, b, jnp.where(lane < 96, c, d)))


def slopes_of(codes):
    size = jnp.exp2((jnp.abs(codes) - MIDDLE) * (1.0 / FINE))
    return jnp.where(codes == 0.0, 0.0, jnp.where(codes < 0.0, -size, size))


def encode(rows, guess):
    if guess is None:
        slope_code = jnp.zeros((ROWS, 1), f32)
        rest = rows
    else:
        over = jnp.sum(rows * guess, axis=1, keepdims=True)
        under = jnp.sum(guess * guess, axis=1, keepdims=True)
        slope = over / jnp.maximum(under, 1e-37)
        size = jnp.maximum(jnp.abs(slope), 1e-30)
        code = jnp.round(jnp.clip(jnp.log2(size) * FINE, -16000.0, 16000.0)) + MIDDLE
        code = jnp.minimum(code, 32000.0)
        slope_code = jnp.where(jnp.abs(slope) < 1e-30, 0.0, jnp.where(slope < 0.0, -code, code))
        rest = rows - slopes_of(slope_code) * guess
    largest = jnp.max(jnp.abs(rest), axis=1, keepdims=True)
    scale_code = jnp.ceil(jnp.log2(jnp.maximum(largest, 1e-34) * (1.0 / 32700.0)) * STEPS)
    coded = jnp.round(rest * jnp.exp2(scale_code * (-1.0 / STEPS)))
    coded = jnp.clip(coded, -32767.0, 32767.0).astype(jnp.int32).astype(i16)
    side = lane_groups(scale_code[:HALF], slope_code[:HALF], scale_code[HALF:], slope_code[HALF:])
    return coded, side.astype(jnp.int32).astype(i16)


def put(out, index, coded, side):
    for b in range(CHUNKS):
        out[index, b * ROWS : (b + 1) * ROWS, :] = coded[:, b * LANES : (b + 1) * LANES]
    out[index, BODY:, :] = side


def decode(message, index, guess):
    side = message[index, BODY:, :].astype(jnp.int32).astype(f32)
    scales = jnp.exp2(side * (1.0 / STEPS))
    scale = jnp.concatenate([scales[:, 0:1], scales[:, 64:65]], axis=0)
    parts = [message[index, b * ROWS : (b + 1) * ROWS, :].astype(jnp.int32).astype(f32) for b in range(CHUNKS)]
    rows = jnp.concatenate(parts, axis=1) * scale
    if guess is not None:
        slopes = slopes_of(side)
        slope = jnp.concatenate([slopes[:, 32:33], slopes[:, 96:97]], axis=0)
        rows = rows + slope * guess
    return rows


def rows_at(d):
    return pl.ds(pl.multiple_of(d * ROWS, ROWS), ROWS)


def live_rows(dims, d):
    at = lax.broadcasted_iota(jnp.int32, (ROWS, N), 0) + d * ROWS
    col = lax.broadcasted_iota(jnp.int32, (ROWS, N), 1)
    return jnp.logical_and(at < dims, col < dims)


def split_kernel(left, right, hop_in, hop_out, back_in, back_out, left2, right2, hop_in2, hop_out2, back):
    for source, target in ((left, left2), (right, right2), (hop_in, hop_in2), (hop_out, hop_out2)):
        target[0], target[1] = two_parts(source[0, 0])
    for at, source in ((0, back_in), (2, back_out)):
        back[at], back[at + 1] = two_parts(source[0, 0].T)


def row_codes(rows):
    largest = jnp.max(jnp.abs(rows), axis=1, keepdims=True)
    scale_code = jnp.ceil(jnp.log2(jnp.maximum(largest, 1e-34) * (1.0 / 32700.0)) * STEPS)
    coded = jnp.round(rows * jnp.exp2(scale_code * (-1.0 / STEPS)))
    return jnp.clip(coded, -32767.0, 32767.0).astype(jnp.int32).astype(i16), scale_code


def pack_kernel(numbers, v_left, v_right, out):
    lane = lax.broadcasted_iota(jnp.int32, (16, LANES), 1)
    side = jnp.zeros((16, LANES), f32)
    coded, scale = row_codes(v_left[0, 0].astype(f32))
    out[0:N, :] = coded
    for g in range(N // 16):
        side = jnp.where(lane // 4 == g, scale[16 * g : 16 * g + 16], side)
    out[2 * N : 2 * N + 16, :] = side.astype(jnp.int32).astype(i16)
    coded, scale = row_codes(v_right[0, 0].astype(f32))
    for b in range(CHUNKS):
        out[N + b * LANES : N + (b + 1) * LANES, :] = coded[:, b * LANES : (b + 1) * LANES]
    side = jnp.zeros((16, LANES), f32)
    for g in range(LANES // 16):
        side = jnp.where(lane // 4 == g, scale[16 * g : 16 * g + 16], side)
    side = side.astype(jnp.int32)
    side = jnp.where(lane >= 64, numbers[1], side)
    out[2 * N + 16 :, :] = jnp.where(lane >= 96, numbers[0], side).astype(i16)


def source_kernel(numbers, packs, everyone, *rest, own):
    if own:
        field, out, low_part, high_part, right = rest
    else:
        field, low_part, high_part, right = rest
    t = pl.program_id(0)
    here = pl.ds(pl.multiple_of(t * LANES, LANES), LANES)
    scales = jnp.exp2(packs[0, 2 * N : 2 * N + 16, :].astype(jnp.int32).astype(f32) * (1.0 / STEPS))
    parts = []
    for g in range(N // 16):
        part = packs[0, 16 * g : 16 * g + 16, :].astype(jnp.int32).astype(f32)
        parts.append((part * scales[:, 4 * g : 4 * g + 1]).astype(bf16))
    tail = packs[0, 2 * N + 16 :, :].astype(jnp.int32).astype(f32)
    lane = lax.broadcasted_iota(jnp.int32, tail.shape, 1)
    link = jnp.max(jnp.where(lane < 64, 0.0, jnp.where(lane < 96, tail, 0.0))).astype(jnp.int32)
    middle = product(jnp.concatenate(parts, axis=0), everyone[link])
    high, low = two_parts(middle)
    high_part[:, here] = high
    low_part[:, here] = low
    scales = jnp.exp2(tail * (1.0 / STEPS))
    scale = jnp.concatenate([scales[:, 4 * g : 4 * g + 1] for g in range(LANES // 16)], axis=0)
    for b in range(CHUNKS):
        part = packs[0, N + b * LANES : N + (b + 1) * LANES, :].astype(jnp.int32).astype(f32)
        right[here, b * LANES : (b + 1) * LANES] = (part * scale).astype(bf16)

    @pl.when(t == PEERS // 2 - 1)
    def _():
        field[...] = product(high_part[...], right[...]) + product(low_part[...], right[...])
        dims = jnp.max(jnp.where(lane < 96, 0.0, tail)).astype(jnp.int32)

        def one(d, carry):
            rows = jnp.where(live_rows(dims, d), -field[rows_at(d), :], 0.0)
            field[rows_at(d), :] = rows
            if own:
                put(out, d, *encode(rows, None))
            return carry

        lax.fori_loop(0, PEERS, one, 0, unroll=4)


def sum_kernel(numbers, messages, first, second, out):
    for c, mine in ((0, first), (1, second)):
        guess = mine[0]
        total = level_gap * guess
        for t in range(PEERS // 2):
            total = total + decode(messages, 2 * t + c, guess)
        put(out, c, *encode(total, guess))


def dots_kernel(numbers, messages, mine, out, own):
    core = numbers[3]

    def one(d, carry):
        rr, rw = carry
        r = mine[0, rows_at(d), :]
        w = decode(messages, 2 * d + core, r)
        own[d] = messages[2 * d + core]
        return rr + r * r, rw + r * w

    zero = jnp.zeros((ROWS, N), f32)
    rr, rw = lax.fori_loop(0, PEERS, one, (zero, zero), unroll=4)
    row = lax.broadcasted_iota(jnp.int32, (8, LANES), 0)
    tile = jnp.where(row == 0, jnp.sum(rr), jnp.where(row == 1, jnp.sum(rw), 0.0))
    out[...] = jnp.broadcast_to(tile[None], out.shape)


def steps_of(totals, past, first):
    total = jnp.sum(totals[...], axis=0)
    norm, along = total[0:1], total[1:2]
    if first:
        ratio = jnp.zeros_like(norm)
        step = norm / along
        back = ratio
    else:
        ratio = norm / past[0:1]
        step = norm / (along - ratio * norm / past[1:2])
        back = step * ratio / past[1:2]
    wide = lambda a: jnp.broadcast_to(a[:, 0:1], (ROWS, N))
    return norm, ratio, step, wide(step), wide(back)


def apply_kernel(numbers, messages, far, *rest, count):
    if count == 0:
        (partner, left, right, hop_in, hop_out, back_ops, r_out, out, halves, mids, image) = rest
    elif count == 1:
        (r_now, totals, left, right, hop_in, hop_out, back_ops, r_out, out, past_out, halves, mids, image) = rest
    else:
        (r_now, totals, r_old, past, left, right, hop_in, hop_out, back_ops, r_out, out, past_out, halves, mids, image) = rest
    if count > 0:
        was = None if count == 1 else past[...]
        norm, ratio, step, wide_step, wide_back = steps_of(totals, was, count == 1)
        row = lax.broadcasted_iota(jnp.int32, (8, LANES), 0)
        tile = jnp.where(row == 0, norm, jnp.where(row == 1, step, 0.0))
        if count == 1:
            tile = jnp.where(row == 2, step, tile)
        else:
            tile = jnp.where(row == 2, was[2:3], jnp.where(row == 3, step, jnp.where(row == 4, ratio, tile)))
        past_out[...] = tile
    core = numbers[3]
    other = partner if count == 0 else messages
    for j, message, stride, first in ((1, messages, 2, core), (2 - 2 * core, other, 2, 1 - core), (2 * core, far, 1, 0)):

        def one(d, carry, j=j, message=message, stride=stride, first=first):
            at = rows_at(d)
            if count == 0:
                r = decode(message, d, None) if stride == 1 else message[at, :]
            else:
                r = r_now[j, at, :]
                w = decode(message, stride * d + first, r)
                new = r - wide_step * w
                if count > 1:
                    new = new - wide_back * (r_old[j, at, :] - r)
                r = new
            r_out[j, at, :] = r
            high, low = two_parts(r)
            halves[j, 0, at, :] = high
            halves[j, 1, at, :] = low
            return carry

        lax.fori_loop(0, PEERS, one, 0, unroll=4)
    pairs = (
        (1, left[0], left[1], right[0], right[1]),
        (2, hop_in[0], hop_in[1], hop_out[0], hop_out[1]),
        (0, back_ops[0], back_ops[1], back_ops[2], back_ops[3]),
    )
    for k, (j, a_high, a_low, b_high, b_low) in enumerate(pairs):
        v_high, v_low = halves[j, 0], halves[j, 1]
        middle = product(a_high, v_high) + (product(a_high, v_low) + product(a_low, v_high))
        m_high, m_low = two_parts(middle)
        mids[0], mids[1] = m_high, m_low
        add = product(mids[0], b_high) + (product(mids[0], b_low) + product(mids[1], b_high))
        image[...] = add if k == 0 else image[...] + add
    dims = numbers[0]

    def send(d, carry):
        at = rows_at(d)
        rows = jnp.where(live_rows(dims, d), image[at, :], 0.0)
        put(out, d, *encode(rows, r_out[1, at, :]))
        return carry

    lax.fori_loop(0, PEERS, send, 0, unroll=4)


def last_kernel(numbers, messages, r0, r1, r2, totals, past, solution, residual):
    core = numbers[3]
    was = past[...]
    norm, ratio, step, wide_step, wide_back = steps_of(totals, was, False)
    step0, step1, ratio1 = was[2:3], was[3:4], was[4:5]
    wide = lambda a: jnp.broadcast_to(a[:, 0:1], (ROWS, N))
    on2 = wide_step
    on1 = wide(step1 + step * ratio)
    on0 = wide(step0 + (step1 + step * ratio) * ratio1)

    def one(d, carry):
        at = rows_at(d)
        a, b, c = r0[0, at, :], r1[0, at, :], r2[0, at, :]
        w = decode(messages, 2 * d + core, c)
        solution[0, at, :] = on0 * a + on1 * b + on2 * c
        residual[0, at, :] = c - wide_step * w - wide_back * (b - c)
        return carry

    lax.fori_loop(0, PEERS, one, 0, unroll=4)


smem = pl.BlockSpec(memory_space=pltpu.SMEM)
vmem = pl.BlockSpec(memory_space=pltpu.VMEM)
params = pltpu.CompilerParams(vmem_limit_bytes=24 * 2**20)
message_shape = jax.ShapeDtypeStruct((PEERS, MESSAGE, LANES), i16)
spread_shape = jax.ShapeDtypeStruct((2, MESSAGE, LANES), i16)
field3 = jax.ShapeDtypeStruct((3, N, N), f32)
small = jax.ShapeDtypeStruct((8, LANES), f32)
whole = jax.ShapeDtypeStruct((1, N, N), f32)


def block(shape, index):
    return pl.BlockSpec(shape, index)


def exchange(messages):
    return lax.all_to_all(messages, GROUP, 0, 0, tiled=True)


def body(left_ops, right_ops, hop_left, hop_right, v_left, v_right, zero_blocks, links, block_dims):
    core = lax.axis_index("core")
    place = lax.axis_index("term") * 2 + core
    count = lax.axis_size(SECTOR)
    everyone = lax.all_to_all(jnp.broadcast_to(zero_blocks, (count, 128, 128)), SECTOR, 0, 0, tiled=True)
    back_in, back_out = shifted(hop_left, SECTOR, 1), shifted(hop_right, SECTOR, 1)
    numbers = jnp.stack([block_dims[0], links[0, 0], place, core]).astype(jnp.int32)

    fixed = lambda rank: (lambda i, n: (0,) * rank)
    pack = pl.pallas_call(
        pack_kernel, out_shape=jax.ShapeDtypeStruct((PACK, LANES), i16), in_specs=[smem, vmem, vmem], out_specs=vmem,
        compiler_params=params, name="pack",
    )(numbers, v_left, v_right)

    def spread(rows):
        return lax.all_gather(rows, GROUP, axis=0, tiled=True)

    def across(own):
        pairs = [(i, i + 1) for i in range(1, count - 1, 2)]
        return lax.ppermute(own, SECTOR, pairs + [(b, a) for a, b in pairs])

    packs = spread(pack[None])

    def source(own):
        shapes = (jax.ShapeDtypeStruct((N, N), f32),) + ((message_shape,) if own else ())
        which = (lambda n: n[3]) if own else (lambda n: 1 - n[3])
        return pl.pallas_call(
            lambda *refs: source_kernel(*refs, own=own), out_shape=shapes,
            grid_spec=pltpu.PrefetchScalarGridSpec(
                num_scalar_prefetch=1, grid=(PEERS // 2,),
                in_specs=[block((1, PACK, LANES), lambda t, n: (2 * t + which(n), 0, 0)), block(everyone.shape, fixed(3))],
                out_specs=tuple(block(shape.shape, fixed(len(shape.shape))) for shape in shapes),
                scratch_shapes=[pltpu.VMEM((N, PEERS // 2 * LANES), bf16)] * 2 + [pltpu.VMEM((PEERS // 2 * LANES, N), bf16)],
            ),
            compiler_params=params, name="source",
        )(numbers, packs, everyone)

    def summed(messages, fields):
        specs = [block((1, ROWS, N), lambda i, n, c=c: (1 + c - n[3], n[2], 0)) for c in (0, 1)]
        return pl.pallas_call(
            sum_kernel, out_shape=spread_shape,
            grid_spec=pltpu.PrefetchScalarGridSpec(
                num_scalar_prefetch=1, grid=(1,),
                in_specs=[block((PEERS, MESSAGE, LANES), fixed(3))] + specs,
                out_specs=block((2, MESSAGE, LANES), fixed(3)),
            ),
            compiler_params=params, name="sum",
        )(numbers, messages, fields, fields)

    def dots(messages, fields):
        return pl.pallas_call(
            dots_kernel, out_shape=(jax.ShapeDtypeStruct((count, 8, LANES), f32), message_shape),
            grid_spec=pltpu.PrefetchScalarGridSpec(
                num_scalar_prefetch=1, grid=(1,),
                in_specs=[block((2 * PEERS, MESSAGE, LANES), fixed(3)), block((1, N, N), lambda i, n: (1, 0, 0))],
                out_specs=(block((count, 8, LANES), fixed(3)), block((PEERS, MESSAGE, LANES), fixed(3))),
            ),
            compiler_params=params, name="dots",
        )(numbers, messages, fields)

    def applied(step, messages, far, extra):
        shapes = (field3, message_shape) + ((small,) if step else ())
        return pl.pallas_call(
            lambda *refs: apply_kernel(*refs, count=step), out_shape=shapes,
            in_specs=[smem] + [vmem] * (2 + len(extra) + 5), out_specs=(vmem,) * len(shapes),
            scratch_shapes=[pltpu.VMEM((3, 2, N, N), bf16), pltpu.VMEM((2, N, N), bf16), pltpu.VMEM((N, N), f32)],
            compiler_params=params, name="apply",
        )(numbers, messages, far, *extra, left, right, hop_in, hop_out, back)

    mine, own = source(True)
    far = across(own)
    back_out, mine = lax.optimization_barrier((back_out, mine))
    messages, extra = mine, tuple(source(False))
    pair = jax.ShapeDtypeStruct((2, N, N), bf16)
    four = jax.ShapeDtypeStruct((4, N, N), bf16)
    left, right, hop_in, hop_out, back = pl.pallas_call(
        split_kernel, out_shape=(pair, pair, pair, pair, four), in_specs=[vmem] * 6, out_specs=(vmem,) * 5,
        compiler_params=params, name="split",
    )(left_ops, right_ops, hop_left, hop_right, back_in, back_out)
    fields, past = [], None
    for step in range(3):
        if step:
            partial, own = dots(messages, fields[-1])
            far = across(own)
            totals = lax.all_to_all(partial, SECTOR, 0, 0, tiled=True)
            extra = (fields[-1], totals) + (() if step == 1 else (fields[-2], past))
        now, rows, *tail = applied(step, messages, far, extra)
        fields.append(now)
        past = tail[0] if tail else None
        messages = spread(summed(exchange(rows), now))
    totals = lax.all_to_all(dots(messages, fields[-1])[0], SECTOR, 0, 0, tiled=True)
    return tuple(
        pl.pallas_call(
            last_kernel, out_shape=(whole, whole),
            grid_spec=pltpu.PrefetchScalarGridSpec(
                num_scalar_prefetch=1, grid=(1,),
                in_specs=[block((2 * PEERS, MESSAGE, LANES), fixed(3))] + [block((1, N, N), lambda i, n: (1, 0, 0))] * 3
                + [block((count, 8, LANES), fixed(3)), block((8, LANES), fixed(2))],
                out_specs=(block((1, N, N), fixed(3)),) * 2,
            ),
            compiler_params=params, name="last",
        )(numbers, messages, *fields, totals, past)
    )


def solution(mesh):
    finer = Mesh(mesh.devices.reshape(mesh.shape["term"], 4, 4, 2), ("term", "sector_0", "sector_1", "core"))
    both = P("term", SECTOR, None, None)
    in_specs = (both,) * 6 + (P(SECTOR, None, None), P("term", SECTOR), P(SECTOR))
    out_specs = (P(SECTOR, None, None), P(SECTOR, None, None))
    return jax.shard_map(body, mesh=finer, in_specs=in_specs, out_specs=out_specs, check_vma=False)
```

```python
import jax
import jax.numpy as jnp
from jax import lax
from jax.experimental import pallas as pl
from jax.experimental.pallas import tpu as pltpu
from jax.sharding import Mesh
from jax.sharding import PartitionSpec as P

SECTOR = ("sector_0", "sector_1", "core")
GROUP = ("term", "core")

level_gap = 2.5
N = 512
LANES = 128
PEERS = 16
ROWS = N // PEERS
CHUNKS = N // LANES
BODY = ROWS * CHUNKS
MESSAGE = BODY + 16
PACK = 2 * N + 32
PARTS = 4
HALF = ROWS // 2
STEPS = 8.0
FINE = 64.0
MIDDLE = 16384.0

f32, bf16, i16 = jnp.float32, jnp.bfloat16, jnp.int16


def shifted(value, axis, steps):
    count = lax.axis_size(axis)
    first, last = (max(0, -steps), min(count, count - steps))
    return lax.ppermute(value, axis, [(source, source + steps) for source in range(first, last)])


def two_parts(value):
    high = value.astype(bf16)
    return high, (value - high.astype(f32)).astype(bf16)


def product(a, b):
    return jnp.dot(a, b, preferred_element_type=f32)


def lane_groups(a, b, c, d):
    lane = lax.broadcasted_iota(jnp.int32, (HALF, LANES), 1)
    return jnp.where(lane < 16, a, jnp.where(lane < 32, b, jnp.where(lane < 48, c, jnp.where(lane < 64, d, 0.0))))


def slopes_of(codes):
    size = jnp.exp2((jnp.abs(codes) - MIDDLE) * (1.0 / FINE))
    return jnp.where(codes == 0.0, 0.0, jnp.where(codes < 0.0, -size, size))


def encode(rows, guess):
    if guess is None:
        slope_code = jnp.zeros((ROWS, 1), f32)
        rest = rows
    else:
        over = jnp.sum(rows * guess, axis=1, keepdims=True)
        under = jnp.sum(guess * guess, axis=1, keepdims=True)
        slope = over / jnp.maximum(under, 1e-37)
        size = jnp.maximum(jnp.abs(slope), 1e-30)
        code = jnp.round(jnp.clip(jnp.log2(size) * FINE, -16000.0, 16000.0)) + MIDDLE
        code = jnp.minimum(code, 32000.0)
        slope_code = jnp.where(jnp.abs(slope) < 1e-30, 0.0, jnp.where(slope < 0.0, -code, code))
        rest = rows - slopes_of(slope_code) * guess
    largest = jnp.max(jnp.abs(rest), axis=1, keepdims=True)
    scale_code = jnp.ceil(jnp.log2(jnp.maximum(largest, 1e-34) * (1.0 / 32700.0)) * STEPS)
    coded = jnp.round(rest * jnp.exp2(scale_code * (-1.0 / STEPS)))
    coded = jnp.clip(coded, -32767.0, 32767.0).astype(jnp.int32).astype(i16)
    side = lane_groups(scale_code[:HALF], slope_code[:HALF], scale_code[HALF:], slope_code[HALF:])
    return coded, side.astype(jnp.int32).astype(i16)


def put(out, index, coded, side):
    for b in range(CHUNKS):
        out[index, b * ROWS : (b + 1) * ROWS, :] = coded[:, b * LANES : (b + 1) * LANES]
    out[index, BODY:, :] = side


def decode(message, index, guess):
    side = message[index, BODY:, :].astype(jnp.int32).astype(f32)
    scales = jnp.exp2(side * (1.0 / STEPS))
    scale = jnp.concatenate([scales[:, 0:1], scales[:, 32:33]], axis=0)
    parts = [message[index, b * ROWS : (b + 1) * ROWS, :].astype(jnp.int32).astype(f32) for b in range(CHUNKS)]
    rows = jnp.concatenate(parts, axis=1) * scale
    if guess is not None:
        slopes = slopes_of(side)
        slope = jnp.concatenate([slopes[:, 16:17], slopes[:, 48:49]], axis=0)
        rows = rows + slope * guess
    return rows


def rows_at(d):
    return pl.ds(pl.multiple_of(d * ROWS, ROWS), ROWS)


def live_rows(dims, d):
    at = lax.broadcasted_iota(jnp.int32, (ROWS, N), 0) + d * ROWS
    col = lax.broadcasted_iota(jnp.int32, (ROWS, N), 1)
    return jnp.logical_and(at < dims, col < dims)


def split_kernel(left, right, hop_in, hop_out, back_in, back_out, left2, right2, hops):
    for source, target in ((left, left2), (right, right2)):
        target[0], target[1] = two_parts(source[0, 0])
    for at, source in ((0, hop_in), (2, hop_out)):
        hops[0, at], hops[0, at + 1] = two_parts(source[0, 0])
    for at, source in ((0, back_in), (2, back_out)):
        hops[1, at], hops[1, at + 1] = two_parts(source[0, 0].T)


def row_codes(rows):
    largest = jnp.max(jnp.abs(rows), axis=1, keepdims=True)
    scale_code = jnp.ceil(jnp.log2(jnp.maximum(largest, 1e-34) * (1.0 / 32700.0)) * STEPS)
    coded = jnp.round(rows * jnp.exp2(scale_code * (-1.0 / STEPS)))
    return jnp.clip(coded, -32767.0, 32767.0).astype(jnp.int32).astype(i16), scale_code


def pack_kernel(numbers, v_left, v_right, out):
    lane = lax.broadcasted_iota(jnp.int32, (16, LANES), 1)
    side = jnp.zeros((16, LANES), f32)
    coded, scale = row_codes(v_left[0, 0].astype(f32))
    out[0:N, :] = coded
    for g in range(N // 16):
        side = jnp.where(lane // 4 == g, scale[16 * g : 16 * g + 16], side)
    out[2 * N : 2 * N + 16, :] = side.astype(jnp.int32).astype(i16)
    coded, scale = row_codes(v_right[0, 0].astype(f32))
    for b in range(CHUNKS):
        out[N + b * LANES : N + (b + 1) * LANES, :] = coded[:, b * LANES : (b + 1) * LANES]
    side = jnp.zeros((16, LANES), f32)
    for g in range(LANES // 16):
        side = jnp.where(lane // 4 == g, scale[16 * g : 16 * g + 16], side)
    side = side.astype(jnp.int32)
    side = jnp.where(lane >= 64, numbers[1], side)
    out[2 * N + 16 :, :] = jnp.where(lane >= 96, numbers[0], side).astype(i16)


def source_kernel(numbers, packs, everyone, *rest, own):
    if own:
        field, out, low_part, high_part, right = rest
    else:
        field, low_part, high_part, right = rest
    t = pl.program_id(0)
    here = pl.ds(pl.multiple_of(t * LANES, LANES), LANES)
    scales = jnp.exp2(packs[0, 2 * N : 2 * N + 16, :].astype(jnp.int32).astype(f32) * (1.0 / STEPS))
    parts = []
    for g in range(N // 16):
        part = packs[0, 16 * g : 16 * g + 16, :].astype(jnp.int32).astype(f32)
        parts.append((part * scales[:, 4 * g : 4 * g + 1]).astype(bf16))
    tail = packs[0, 2 * N + 16 :, :].astype(jnp.int32).astype(f32)
    lane = lax.broadcasted_iota(jnp.int32, tail.shape, 1)
    link = jnp.max(jnp.where(lane < 64, 0.0, jnp.where(lane < 96, tail, 0.0))).astype(jnp.int32)
    middle = product(jnp.concatenate(parts, axis=0), everyone[link])
    high, low = two_parts(middle)
    high_part[:, here] = high
    low_part[:, here] = low
    scales = jnp.exp2(tail * (1.0 / STEPS))
    scale = jnp.concatenate([scales[:, 4 * g : 4 * g + 1] for g in range(LANES // 16)], axis=0)
    for b in range(CHUNKS):
        part = packs[0, N + b * LANES : N + (b + 1) * LANES, :].astype(jnp.int32).astype(f32)
        right[here, b * LANES : (b + 1) * LANES] = (part * scale).astype(bf16)

    @pl.when(t == PEERS // 2 - 1)
    def _():
        field[...] = product(high_part[...], right[...]) + product(low_part[...], right[...])
        dims = jnp.max(jnp.where(lane < 96, 0.0, tail)).astype(jnp.int32)

        def one(d, carry):
            rows = jnp.where(live_rows(dims, d), -field[rows_at(d), :], 0.0)
            field[rows_at(d), :] = rows
            if own:
                put(out, d, *encode(rows, None))
            return carry

        lax.fori_loop(0, PEERS, one, 0, unroll=4)


def write_share(out, share):
    value = jnp.full((16, LANES), share, f32)
    power = jnp.ceil(jnp.log2(jnp.maximum(jnp.abs(value), 1e-30)))
    scaled = value * jnp.exp2(-power) * MIDDLE
    coarse = jnp.round(scaled)
    fine = jnp.round((scaled - coarse) * (2.0 * MIDDLE))
    lane = lax.broadcasted_iota(jnp.int32, (16, LANES), 1)
    codes = jnp.where(lane < 80, power, jnp.where(lane < 96, coarse, fine)).astype(jnp.int32)
    for d in range(PEERS):
        out[d, BODY:, :] = jnp.where(lane < 64, out[d, BODY:, :].astype(jnp.int32), codes).astype(i16)


def read_share(messages, index):
    side = messages[index, BODY:, :].astype(jnp.int32).astype(f32)[0:8]
    return (side[:, 80:81] + side[:, 96:97] * (0.5 / MIDDLE)) * jnp.exp2(side[:, 64:65]) * (1.0 / MIDDLE)


def sum_kernel(numbers, messages, first, second, norm, out, sums):
    core = numbers[3]
    share = jnp.zeros((8, 1), f32)
    for t in range(PEERS // 2):
        share = share + read_share(messages, 2 * t + core)
    row = lax.broadcasted_iota(jnp.int32, (8, LANES), 0)
    tile = jnp.where(row == 0, norm[...], jnp.where(row == 1, level_gap * norm[...] + share, 0.0))
    sums[...] = jnp.broadcast_to(tile[None], sums.shape)
    for c, mine in ((0, first), (1, second)):
        guess = mine[0]
        total = level_gap * guess
        for t in range(PEERS // 2):
            total = total + decode(messages, 2 * t + c, guess)
        put(out, c, *encode(total, guess))


def steps_of(totals, past, first):
    total = jnp.sum(totals[...], axis=0)
    norm, along = total[0:1], total[1:2]
    if first:
        ratio = jnp.zeros_like(norm)
        step = norm / along
        back = ratio
    else:
        ratio = norm / past[0:1]
        step = norm / (along - ratio * norm / past[1:2])
        back = step * ratio / past[1:2]
    wide = lambda a: jnp.broadcast_to(a[:, 0:1], (ROWS, N))
    return norm, ratio, step, wide(step), wide(back)


def times(image, mids, ops, at, v_high, v_low, right, out_at, keep):
    a_high, a_low, b_high, b_low = ops[at], ops[at + 1], right[out_at], right[out_at + 1]
    middle = product(a_high, v_high) + (product(a_high, v_low) + product(a_low, v_high))
    mids[0], mids[1] = two_parts(middle)
    add = product(mids[0], b_high) + (product(mids[0], b_low) + product(mids[1], b_high))
    image[...] = image[...] + add if keep else add


def near_kernel(numbers, *rest, count):
    if count == 0:
        (mine, partner, left_at, right_at, hops_at, r_out, image, norm_out, *scratch) = rest
    elif count == 1:
        (messages_at, r_now, totals, left_at, right_at, hops_at, r_out, image, norm_out, past_out, *scratch) = rest
    else:
        (messages_at, r_now, totals, r_old_at, past, left_at, right_at, hops_at, r_out, image, norm_out, past_out, *scratch) = rest
    halves, mids, left, right, hops, sems, *held = scratch
    core = numbers[3]
    loads = [
        pltpu.make_async_copy(left_at, left, sems.at[0]),
        pltpu.make_async_copy(right_at, right, sems.at[1]),
        pltpu.make_async_copy(hops_at.at[core], hops, sems.at[2]),
    ]
    early = []
    if count > 0:
        messages, arrivals = held[:2]
        for q in range(PARTS):
            piece = pl.ds(q * (2 * PEERS // PARTS), 2 * PEERS // PARTS)
            early.append([pltpu.make_async_copy(messages_at.at[piece], messages.at[piece], arrivals.at[0, q])])
            if count > 1:
                r_old = held[2]
                piece = pl.ds(q * (N // PARTS), N // PARTS)
                early[q].append(pltpu.make_async_copy(r_old_at.at[:, piece], r_old.at[:, piece], arrivals.at[1, q]))
    for load in sum(early, []) + loads:
        load.start()
    if count > 0:
        was = None if count == 1 else past[...]
        norm, ratio, step, wide_step, wide_back = steps_of(totals, was, count == 1)
        row = lax.broadcasted_iota(jnp.int32, (8, LANES), 0)
        tile = jnp.where(row == 0, norm, jnp.where(row == 1, step, 0.0))
        if count == 1:
            tile = jnp.where(row == 2, step, tile)
        else:
            tile = jnp.where(row == 2, was[2:3], jnp.where(row == 3, step, jnp.where(row == 4, ratio, tile)))
        past_out[...] = tile
    square = jnp.zeros((ROWS, N), f32)
    for j in (0, 1):

        def one(d, square, j=j):
            at = rows_at(d)
            if count == 0:
                r = (mine, partner)[j][at, :]
            else:
                r = r_now[j, at, :]
                w = decode(messages, 2 * d + (core if j == 0 else 1 - core), r)
                new = r - wide_step * w
                if count > 1:
                    new = new - wide_back * (r_old[j, at, :] - r)
                r = new
            r_out[j, at, :] = r
            high, low = two_parts(r)
            halves[j, 0, at, :] = high
            halves[j, 1, at, :] = low
            return square + r * r if j == 0 else square

        for q in range(PARTS):
            if j == 0 and count > 0:
                for load in early[q]:
                    load.wait()
            square = lax.fori_loop(q * (PEERS // PARTS), (q + 1) * (PEERS // PARTS), one, square, unroll=4)
    norm_out[...] = jnp.full((8, LANES), jnp.sum(square), f32)
    loads[0].wait()
    loads[1].wait()
    times(image, mids, left, 0, halves[0, 0], halves[0, 1], right, 0, False)
    loads[2].wait()
    times(image, mids, hops, 0, halves[1, 0], halves[1, 1], hops, 2, True)


def far_kernel(numbers, far, near, image_in, *rest, count):
    if count == 0:
        (hops_at, r_out, out, *scratch) = rest
    elif count == 1:
        (r_now, totals, hops_at, r_out, out, *scratch) = rest
    else:
        (r_now, totals, r_old, past, hops_at, r_out, out, *scratch) = rest
    halves, mids, image, hops, sem = scratch
    core = numbers[3]
    load = pltpu.make_async_copy(hops_at.at[1 - core], hops, sem)
    load.start()
    if count > 0:
        was = None if count == 1 else past[...]
        _, _, _, wide_step, wide_back = steps_of(totals, was, count == 1)

    def one(d, carry):
        at = rows_at(d)
        if count == 0:
            r = decode(far, d, None)
        else:
            r = r_now[at, :]
            new = r - wide_step * decode(far, d, r)
            if count > 1:
                new = new - wide_back * (r_old[at, :] - r)
            r = new
        r_out[at, :] = r
        high, low = two_parts(r)
        halves[0, at, :] = high
        halves[1, at, :] = low
        return carry

    lax.fori_loop(0, PEERS, one, 0, unroll=4)
    load.wait()
    times(image, mids, hops, 0, halves[0], halves[1], hops, 2, False)
    dims = numbers[0]

    def send(d, share):
        at = rows_at(d)
        r = near[0, at, :]
        rows = jnp.where(live_rows(dims, d), image[at, :] + image_in[at, :], 0.0)
        put(out, d, *encode(rows, r))
        return share + rows * r

    share = lax.fori_loop(0, PEERS, send, jnp.zeros((ROWS, N), f32), unroll=4)
    write_share(out, jnp.sum(share))


def last_kernel(numbers, messages, r0_at, r1_at, r2, totals, past, solution, residual, r0, r1, sems):
    core = numbers[3]
    loads = [pltpu.make_async_copy(r1_at.at[pl.ds(0, 1)], r1, sems.at[0]), pltpu.make_async_copy(r0_at.at[pl.ds(0, 1)], r0, sems.at[1])]
    for load in loads:
        load.start()
    was = past[...]
    norm, ratio, step, wide_step, wide_back = steps_of(totals, was, False)
    step0, step1, ratio1 = was[2:3], was[3:4], was[4:5]
    wide = lambda a: jnp.broadcast_to(a[:, 0:1], (ROWS, N))
    on2 = wide_step
    on1 = wide(step1 + step * ratio)
    on0 = wide(step0 + (step1 + step * ratio) * ratio1)
    for load in loads:
        load.wait()

    def one(d, carry):
        at = rows_at(d)
        a, b, c = r0[0, at, :], r1[0, at, :], r2[0, at, :]
        w = decode(messages, 2 * d + core, c)
        solution[0, at, :] = on0 * a + on1 * b + on2 * c
        residual[0, at, :] = c - wide_step * w - wide_back * (b - c)
        return carry

    lax.fori_loop(0, PEERS, one, 0, unroll=4)


smem = pl.BlockSpec(memory_space=pltpu.SMEM)
vmem = pl.BlockSpec(memory_space=pltpu.VMEM)
anywhere = pl.BlockSpec(memory_space=pltpu.HBM)
params = pltpu.CompilerParams(vmem_limit_bytes=24 * 2**20)
message_shape = jax.ShapeDtypeStruct((PEERS, MESSAGE, LANES), i16)
spread_shape = jax.ShapeDtypeStruct((2, MESSAGE, LANES), i16)
small = jax.ShapeDtypeStruct((8, LANES), f32)
whole = jax.ShapeDtypeStruct((1, N, N), f32)


def block(shape, index):
    return pl.BlockSpec(shape, index)


def exchange(messages):
    return lax.all_to_all(messages, GROUP, 0, 0, tiled=True)


def stay(value):
    return pltpu.with_memory_space_constraint(value, pltpu.HBM)


def body(left_ops, right_ops, hop_left, hop_right, v_left, v_right, zero_blocks, links, block_dims):
    core = lax.axis_index("core")
    place = lax.axis_index("term") * 2 + core
    count = lax.axis_size(SECTOR)
    everyone = lax.all_to_all(jnp.broadcast_to(zero_blocks, (count, 128, 128)), SECTOR, 0, 0, tiled=True)
    back_in, back_out = shifted(hop_left, SECTOR, 1), shifted(hop_right, SECTOR, 1)
    numbers = jnp.stack([block_dims[0], links[0, 0], place, core]).astype(jnp.int32)

    fixed = lambda rank: (lambda i, n: (0,) * rank)
    pack = pl.pallas_call(
        pack_kernel, out_shape=jax.ShapeDtypeStruct((PACK, LANES), i16), in_specs=[smem, vmem, vmem], out_specs=vmem,
        compiler_params=params, name="pack",
    )(numbers, v_left, v_right)

    def spread(rows):
        return lax.all_gather(rows, GROUP, axis=0, tiled=True)

    def across(own):
        pairs = [(i, i + 1) for i in range(1, count - 1, 2)]
        return lax.ppermute(own, SECTOR, pairs + [(b, a) for a, b in pairs])

    packs = spread(pack[None])

    def source(own):
        shapes = (jax.ShapeDtypeStruct((N, N), f32),) + ((message_shape,) if own else ())
        which = (lambda n: n[3]) if own else (lambda n: 1 - n[3])
        return pl.pallas_call(
            lambda *refs: source_kernel(*refs, own=own), out_shape=shapes,
            grid_spec=pltpu.PrefetchScalarGridSpec(
                num_scalar_prefetch=1, grid=(PEERS // 2,),
                in_specs=[block((1, PACK, LANES), lambda t, n: (2 * t + which(n), 0, 0)), block(everyone.shape, fixed(3))],
                out_specs=tuple(block(shape.shape, fixed(len(shape.shape))) for shape in shapes),
                scratch_shapes=[pltpu.VMEM((N, PEERS // 2 * LANES), bf16)] * 2 + [pltpu.VMEM((PEERS // 2 * LANES, N), bf16)],
            ),
            compiler_params=params, name="source",
        )(numbers, stay(packs), everyone)

    def summed(messages, near, norm):
        specs = [block((1, ROWS, N), lambda i, n, c=c: (jnp.where(n[3] == c, 0, 1), n[2], 0)) for c in (0, 1)]
        return pl.pallas_call(
            sum_kernel, out_shape=(spread_shape, jax.ShapeDtypeStruct((count, 8, LANES), f32)),
            grid_spec=pltpu.PrefetchScalarGridSpec(
                num_scalar_prefetch=1, grid=(1,),
                in_specs=[block((PEERS, MESSAGE, LANES), fixed(3))] + specs + [block((8, LANES), fixed(2))],
                out_specs=(block((2, MESSAGE, LANES), fixed(3)), block((count, 8, LANES), fixed(3))),
            ),
            compiler_params=params, name="sum",
        )(numbers, messages, near, near, norm)

    mine, own = source(True)
    far = across(own)
    back_out, mine = lax.optimization_barrier((back_out, mine))
    (partner,) = source(False)
    pair = jax.ShapeDtypeStruct((2, N, N), bf16)
    left, right, hops = pl.pallas_call(
        split_kernel, out_shape=(pair, pair, jax.ShapeDtypeStruct((2, 4, N, N), bf16)), in_specs=[vmem] * 6, out_specs=(vmem,) * 3,
        compiler_params=params, name="split",
    )(left_ops, right_ops, hop_left, hop_right, back_in, back_out)
    field, two = jax.ShapeDtypeStruct((N, N), f32), jax.ShapeDtypeStruct((2, N, N), f32)
    nears, fars, past = [], [], None
    for step in range(3):
        if step == 0:
            given, given_far = (mine, partner), ()
        else:
            own = lax.dynamic_index_in_dim(messages.reshape(PEERS, 2, MESSAGE, LANES), core, 1, keepdims=False)
            far = across(own)
            given = (messages, nears[-1], totals) + (() if step == 1 else (nears[-2], past))
            given_far = (fars[-1], totals) + (() if step == 1 else (fars[-2], past))
        shapes = (two, field, small) + ((small,) if step else ())
        distant = ((), (0,), (0, 3))[step]
        held = [pltpu.VMEM((2 * PEERS, MESSAGE, LANES), i16), pltpu.SemaphoreType.DMA((2, PARTS)), pltpu.VMEM((2, N, N), f32)][: (0, 2, 3)[step]]
        near, image, norm, *tail = pl.pallas_call(
            lambda *refs: near_kernel(*refs, count=step), out_shape=shapes,
            in_specs=[smem] + [anywhere if k in distant else vmem for k in range(len(given))] + [anywhere] * 3, out_specs=(vmem,) * len(shapes),
            scratch_shapes=[pltpu.VMEM((2, 2, N, N), bf16)] + [pltpu.VMEM((2, N, N), bf16)] * 3
            + [pltpu.VMEM((4, N, N), bf16), pltpu.SemaphoreType.DMA((3,))] + held,
            compiler_params=params, name="near",
        )(numbers, *[stay(v) if k in distant else v for k, v in enumerate(given)], stay(left), stay(right), stay(hops))
        away, rows = pl.pallas_call(
            lambda *refs: far_kernel(*refs, count=step), out_shape=(field, message_shape),
            in_specs=[smem] + [vmem] * (len(given_far) + 3) + [anywhere], out_specs=(vmem,) * 2,
            scratch_shapes=[pltpu.VMEM((2, N, N), bf16)] * 2 + [pltpu.VMEM((N, N), f32), pltpu.VMEM((4, N, N), bf16), pltpu.SemaphoreType.DMA],
            compiler_params=params, name="far",
        )(numbers, far, near, image, *given_far, stay(hops))
        nears.append(near)
        fars.append(away)
        past = tail[0] if tail else None
        rows, sums = summed(exchange(rows), near, norm)
        totals = lax.all_to_all(sums, SECTOR, 0, 0, tiled=True)
        messages, totals = lax.optimization_barrier((spread(rows), totals))
    return tuple(
        pl.pallas_call(
            last_kernel, out_shape=(whole, whole),
            grid_spec=pltpu.PrefetchScalarGridSpec(
                num_scalar_prefetch=1, grid=(1,),
                in_specs=[block((2 * PEERS, MESSAGE, LANES), fixed(3))] + [anywhere] * 2 + [block((1, N, N), fixed(3))]
                + [block((count, 8, LANES), fixed(3)), block((8, LANES), fixed(2))],
                out_specs=(block((1, N, N), fixed(3)),) * 2,
                scratch_shapes=[pltpu.VMEM((1, N, N), f32)] * 2 + [pltpu.SemaphoreType.DMA((2,))],
            ),
            compiler_params=params, name="last",
        )(numbers, messages, *[stay(near) for near in nears], totals, past)
    )


def solution(mesh):
    finer = Mesh(mesh.devices.reshape(mesh.shape["term"], 4, 4, 2), ("term", "sector_0", "sector_1", "core"))
    both = P("term", SECTOR, None, None)
    in_specs = (both,) * 6 + (P(SECTOR, None, None), P("term", SECTOR), P(SECTOR))
    out_specs = (P(SECTOR, None, None), P(SECTOR, None, None))
    return jax.shard_map(body, mesh=finer, in_specs=in_specs, out_specs=out_specs, check_vma=False)
```

```python
import jax
import jax.numpy as jnp
from jax import lax
from jax.experimental import pallas as pl
from jax.experimental.pallas import tpu as pltpu
from jax.sharding import Mesh
from jax.sharding import PartitionSpec as P

SECTOR = ("sector_0", "sector_1", "core")
GROUP = ("term", "core")

level_gap = 2.5
N = 512
LANES = 128
PEERS = 16
ROWS = N // PEERS
CHUNKS = N // LANES
BODY = ROWS * CHUNKS
MESSAGE = BODY + 16
PACK = 2 * N + 32
PARTS = 4
HALF = ROWS // 2
STEPS = 8.0
FINE = 64.0
MIDDLE = 16384.0

f32, bf16, i16 = jnp.float32, jnp.bfloat16, jnp.int16


def shifted(value, axis, steps):
    count = lax.axis_size(axis)
    first, last = (max(0, -steps), min(count, count - steps))
    return lax.ppermute(value, axis, [(source, source + steps) for source in range(first, last)])


def two_parts(value):
    high = value.astype(bf16)
    return high, (value - high.astype(f32)).astype(bf16)


def product(a, b):
    return jnp.dot(a, b, preferred_element_type=f32)


def lane_groups(a, b, c, d):
    lane = lax.broadcasted_iota(jnp.int32, (HALF, LANES), 1)
    return jnp.where(lane < 16, a, jnp.where(lane < 32, b, jnp.where(lane < 48, c, jnp.where(lane < 64, d, 0.0))))


def slopes_of(codes):
    size = jnp.exp2((jnp.abs(codes) - MIDDLE) * (1.0 / FINE))
    return jnp.where(codes == 0.0, 0.0, jnp.where(codes < 0.0, -size, size))


def encode(rows, guess):
    if guess is None:
        slope_code = jnp.zeros((ROWS, 1), f32)
        rest = rows
    else:
        over = jnp.sum(rows * guess, axis=1, keepdims=True)
        under = jnp.sum(guess * guess, axis=1, keepdims=True)
        slope = over / jnp.maximum(under, 1e-37)
        size = jnp.maximum(jnp.abs(slope), 1e-30)
        code = jnp.round(jnp.clip(jnp.log2(size) * FINE, -16000.0, 16000.0)) + MIDDLE
        code = jnp.minimum(code, 32000.0)
        slope_code = jnp.where(jnp.abs(slope) < 1e-30, 0.0, jnp.where(slope < 0.0, -code, code))
        rest = rows - slopes_of(slope_code) * guess
    largest = jnp.max(jnp.abs(rest), axis=1, keepdims=True)
    scale_code = jnp.ceil(jnp.log2(jnp.maximum(largest, 1e-34) * (1.0 / 32700.0)) * STEPS)
    coded = jnp.round(rest * jnp.exp2(scale_code * (-1.0 / STEPS)))
    coded = jnp.clip(coded, -32767.0, 32767.0).astype(jnp.int32).astype(i16)
    side = lane_groups(scale_code[:HALF], slope_code[:HALF], scale_code[HALF:], slope_code[HALF:])
    return coded, side.astype(jnp.int32).astype(i16)


def put(out, index, coded, side):
    for b in range(CHUNKS):
        out[index, b * ROWS : (b + 1) * ROWS, :] = coded[:, b * LANES : (b + 1) * LANES]
    out[index, BODY:, :] = side


def decode(message, index, guess):
    side = message[index, BODY:, :].astype(jnp.int32).astype(f32)
    scales = jnp.exp2(side * (1.0 / STEPS))
    scale = jnp.concatenate([scales[:, 0:1], scales[:, 32:33]], axis=0)
    parts = [message[index, b * ROWS : (b + 1) * ROWS, :].astype(jnp.int32).astype(f32) for b in range(CHUNKS)]
    rows = jnp.concatenate(parts, axis=1) * scale
    if guess is not None:
        slopes = slopes_of(side)
        slope = jnp.concatenate([slopes[:, 16:17], slopes[:, 48:49]], axis=0)
        rows = rows + slope * guess
    return rows


def rows_at(d):
    return pl.ds(pl.multiple_of(d * ROWS, ROWS), ROWS)


def live_rows(dims, d):
    at = lax.broadcasted_iota(jnp.int32, (ROWS, N), 0) + d * ROWS
    col = lax.broadcasted_iota(jnp.int32, (ROWS, N), 1)
    return jnp.logical_and(at < dims, col < dims)


def split_kernel(left, right, hop_in, hop_out, back_in, back_out, left2, right2, hop_in2, hop_out2, back):
    for source, target in ((left, left2), (right, right2), (hop_in, hop_in2), (hop_out, hop_out2)):
        target[0], target[1] = two_parts(source[0, 0])
    for at, source in ((0, back_in), (2, back_out)):
        back[at], back[at + 1] = two_parts(source[0, 0].T)


def row_codes(rows):
    largest = jnp.max(jnp.abs(rows), axis=1, keepdims=True)
    scale_code = jnp.ceil(jnp.log2(jnp.maximum(largest, 1e-34) * (1.0 / 32700.0)) * STEPS)
    coded = jnp.round(rows * jnp.exp2(scale_code * (-1.0 / STEPS)))
    return jnp.clip(coded, -32767.0, 32767.0).astype(jnp.int32).astype(i16), scale_code


def pack_kernel(numbers, v_left, v_right, out):
    lane = lax.broadcasted_iota(jnp.int32, (16, LANES), 1)
    side = jnp.zeros((16, LANES), f32)
    coded, scale = row_codes(v_left[0, 0].astype(f32))
    out[0:N, :] = coded
    for g in range(N // 16):
        side = jnp.where(lane // 4 == g, scale[16 * g : 16 * g + 16], side)
    out[2 * N : 2 * N + 16, :] = side.astype(jnp.int32).astype(i16)
    coded, scale = row_codes(v_right[0, 0].astype(f32))
    for b in range(CHUNKS):
        out[N + b * LANES : N + (b + 1) * LANES, :] = coded[:, b * LANES : (b + 1) * LANES]
    side = jnp.zeros((16, LANES), f32)
    for g in range(LANES // 16):
        side = jnp.where(lane // 4 == g, scale[16 * g : 16 * g + 16], side)
    side = side.astype(jnp.int32)
    side = jnp.where(lane >= 64, numbers[1], side)
    out[2 * N + 16 :, :] = jnp.where(lane >= 96, numbers[0], side).astype(i16)


def source_kernel(numbers, packs, everyone, *rest, own):
    if own:
        field, out, low_part, high_part, right = rest
    else:
        field, low_part, high_part, right = rest
    t = pl.program_id(0)
    here = pl.ds(pl.multiple_of(t * LANES, LANES), LANES)
    scales = jnp.exp2(packs[0, 2 * N : 2 * N + 16, :].astype(jnp.int32).astype(f32) * (1.0 / STEPS))
    parts = []
    for g in range(N // 16):
        part = packs[0, 16 * g : 16 * g + 16, :].astype(jnp.int32).astype(f32)
        parts.append((part * scales[:, 4 * g : 4 * g + 1]).astype(bf16))
    tail = packs[0, 2 * N + 16 :, :].astype(jnp.int32).astype(f32)
    lane = lax.broadcasted_iota(jnp.int32, tail.shape, 1)
    link = jnp.max(jnp.where(lane < 64, 0.0, jnp.where(lane < 96, tail, 0.0))).astype(jnp.int32)
    middle = product(jnp.concatenate(parts, axis=0), everyone[link])
    high, low = two_parts(middle)
    high_part[:, here] = high
    low_part[:, here] = low
    scales = jnp.exp2(tail * (1.0 / STEPS))
    scale = jnp.concatenate([scales[:, 4 * g : 4 * g + 1] for g in range(LANES // 16)], axis=0)
    for b in range(CHUNKS):
        part = packs[0, N + b * LANES : N + (b + 1) * LANES, :].astype(jnp.int32).astype(f32)
        right[here, b * LANES : (b + 1) * LANES] = (part * scale).astype(bf16)

    @pl.when(t == PEERS // 2 - 1)
    def _():
        field[...] = product(high_part[...], right[...]) + product(low_part[...], right[...])
        dims = jnp.max(jnp.where(lane < 96, 0.0, tail)).astype(jnp.int32)

        def one(d, carry):
            rows = jnp.where(live_rows(dims, d), -field[rows_at(d), :], 0.0)
            field[rows_at(d), :] = rows
            if own:
                put(out, d, *encode(rows, None))
            return carry

        lax.fori_loop(0, PEERS, one, 0, unroll=4)


def write_share(out, share):
    value = jnp.full((16, LANES), share, f32)
    power = jnp.ceil(jnp.log2(jnp.maximum(jnp.abs(value), 1e-30)))
    scaled = value * jnp.exp2(-power) * MIDDLE
    coarse = jnp.round(scaled)
    fine = jnp.round((scaled - coarse) * (2.0 * MIDDLE))
    lane = lax.broadcasted_iota(jnp.int32, (16, LANES), 1)
    codes = jnp.where(lane < 80, power, jnp.where(lane < 96, coarse, fine)).astype(jnp.int32)
    for d in range(PEERS):
        out[d, BODY:, :] = jnp.where(lane < 64, out[d, BODY:, :].astype(jnp.int32), codes).astype(i16)


def read_share(messages, index):
    side = messages[index, BODY:, :].astype(jnp.int32).astype(f32)[0:8]
    return (side[:, 80:81] + side[:, 96:97] * (0.5 / MIDDLE)) * jnp.exp2(side[:, 64:65]) * (1.0 / MIDDLE)


def sum_kernel(numbers, messages, first, second, *rest):
    if len(rest) == 1:
        (out,) = rest
    else:
        norm, out, sums = rest
        core = numbers[3]
        share = jnp.zeros((8, 1), f32)
        for t in range(PEERS // 2):
            share = share + read_share(messages, 2 * t + core)
        row = lax.broadcasted_iota(jnp.int32, (8, LANES), 0)
        tile = jnp.where(row == 0, norm[...], jnp.where(row == 1, level_gap * norm[...] + share, 0.0))
        sums[...] = jnp.broadcast_to(tile[None], sums.shape)
    for c, mine in ((0, first), (1, second)):
        guess = mine[0]
        total = level_gap * guess
        for t in range(PEERS // 2):
            total = total + decode(messages, 2 * t + c, guess)
        put(out, c, *encode(total, guess))


def dots_kernel(numbers, messages, mine, out, own):
    core = numbers[3]

    def one(d, carry):
        rr, rw = carry
        r = mine[0, rows_at(d), :]
        w = decode(messages, 2 * d + core, r)
        own[d] = messages[2 * d + core]
        return rr + r * r, rw + r * w

    zero = jnp.zeros((ROWS, N), f32)
    rr, rw = lax.fori_loop(0, PEERS, one, (zero, zero), unroll=4)
    row = lax.broadcasted_iota(jnp.int32, (8, LANES), 0)
    tile = jnp.where(row == 0, jnp.sum(rr), jnp.where(row == 1, jnp.sum(rw), 0.0))
    out[...] = jnp.broadcast_to(tile[None], out.shape)


def steps_of(totals, past, first):
    total = jnp.sum(totals[...], axis=0)
    norm, along = total[0:1], total[1:2]
    if first:
        ratio = jnp.zeros_like(norm)
        step = norm / along
        back = ratio
    else:
        ratio = norm / past[0:1]
        step = norm / (along - ratio * norm / past[1:2])
        back = step * ratio / past[1:2]
    wide = lambda a: jnp.broadcast_to(a[:, 0:1], (ROWS, N))
    return norm, ratio, step, wide(step), wide(back)


def apply_kernel(numbers, messages, far, *rest, count):
    if count == 0:
        (partner, left, right, hop_in, hop_out, back_ops, r_out, out, halves, mids, image) = rest
    elif count == 1:
        (r_now, totals, left, right, hop_in, hop_out, back_ops, r_out, out, past_out, halves, mids, image) = rest
    else:
        (r_now, totals, r_old, past, left, right, hop_in, hop_out, back_ops, r_out, out, past_out, norm_out, halves, mids, image) = rest
    if count > 0:
        was = None if count == 1 else past[...]
        norm, ratio, step, wide_step, wide_back = steps_of(totals, was, count == 1)
        row = lax.broadcasted_iota(jnp.int32, (8, LANES), 0)
        tile = jnp.where(row == 0, norm, jnp.where(row == 1, step, 0.0))
        if count == 1:
            tile = jnp.where(row == 2, step, tile)
        else:
            tile = jnp.where(row == 2, was[2:3], jnp.where(row == 3, step, jnp.where(row == 4, ratio, tile)))
        past_out[...] = tile
    core = numbers[3]
    other = partner if count == 0 else messages
    for j, message, stride, first in ((1, messages, 2, core), (2 - 2 * core, other, 2, 1 - core), (2 * core, far, 1, 0)):

        def one(d, carry, j=j, message=message, stride=stride, first=first):
            at = rows_at(d)
            if count == 0:
                r = decode(message, d, None) if stride == 1 else message[at, :]
            else:
                r = r_now[j, at, :]
                w = decode(message, stride * d + first, r)
                new = r - wide_step * w
                if count > 1:
                    new = new - wide_back * (r_old[j, at, :] - r)
                r = new
            r_out[j, at, :] = r
            high, low = two_parts(r)
            halves[j, 0, at, :] = high
            halves[j, 1, at, :] = low
            return carry

        lax.fori_loop(0, PEERS, one, 0, unroll=4)
    pairs = (
        (1, left[0], left[1], right[0], right[1]),
        (2, hop_in[0], hop_in[1], hop_out[0], hop_out[1]),
        (0, back_ops[0], back_ops[1], back_ops[2], back_ops[3]),
    )
    for k, (j, a_high, a_low, b_high, b_low) in enumerate(pairs):
        v_high, v_low = halves[j, 0], halves[j, 1]
        middle = product(a_high, v_high) + (product(a_high, v_low) + product(a_low, v_high))
        m_high, m_low = two_parts(middle)
        mids[0], mids[1] = m_high, m_low
        add = product(mids[0], b_high) + (product(mids[0], b_low) + product(mids[1], b_high))
        image[...] = add if k == 0 else image[...] + add
    dims = numbers[0]

    def send(d, carry):
        at = rows_at(d)
        r = r_out[1, at, :]
        rows = jnp.where(live_rows(dims, d), image[at, :], 0.0)
        put(out, d, *encode(rows, r))
        return (carry[0] + rows * r, carry[1] + r * r) if count == 2 else carry

    zero = jnp.zeros((ROWS, N), f32)
    carry = lax.fori_loop(0, PEERS, send, (zero, zero) if count == 2 else 0, unroll=4)
    if count == 2:
        write_share(out, jnp.sum(carry[0]))
        norm_out[...] = jnp.full((8, LANES), jnp.sum(carry[1]), f32)


def last_kernel(numbers, messages, r0, r1, r2, totals, past, solution, residual):
    core = numbers[3]
    was = past[...]
    norm, ratio, step, wide_step, wide_back = steps_of(totals, was, False)
    step0, step1, ratio1 = was[2:3], was[3:4], was[4:5]
    wide = lambda a: jnp.broadcast_to(a[:, 0:1], (ROWS, N))
    on2 = wide_step
    on1 = wide(step1 + step * ratio)
    on0 = wide(step0 + (step1 + step * ratio) * ratio1)

    for d in range(PEERS // PARTS):
        at = slice(d * ROWS, (d + 1) * ROWS)
        a, b, c = r0[0, at, :], r1[0, at, :], r2[0, at, :]
        w = decode(messages, 2 * d + core, c)
        solution[0, at, :] = on0 * a + on1 * b + on2 * c
        residual[0, at, :] = c - wide_step * w - wide_back * (b - c)


smem = pl.BlockSpec(memory_space=pltpu.SMEM)
vmem = pl.BlockSpec(memory_space=pltpu.VMEM)
params = pltpu.CompilerParams(vmem_limit_bytes=24 * 2**20)
message_shape = jax.ShapeDtypeStruct((PEERS, MESSAGE, LANES), i16)
spread_shape = jax.ShapeDtypeStruct((2, MESSAGE, LANES), i16)
field3 = jax.ShapeDtypeStruct((3, N, N), f32)
small = jax.ShapeDtypeStruct((8, LANES), f32)
whole = jax.ShapeDtypeStruct((1, N, N), f32)


def block(shape, index):
    return pl.BlockSpec(shape, index)


def exchange(messages):
    return lax.all_to_all(messages, GROUP, 0, 0, tiled=True)


def stay(value):
    return pltpu.with_memory_space_constraint(value, pltpu.HBM)


def body(left_ops, right_ops, hop_left, hop_right, v_left, v_right, zero_blocks, links, block_dims):
    core = lax.axis_index("core")
    place = lax.axis_index("term") * 2 + core
    count = lax.axis_size(SECTOR)
    everyone = lax.all_to_all(jnp.broadcast_to(zero_blocks, (count, 128, 128)), SECTOR, 0, 0, tiled=True)
    back_in, back_out = shifted(hop_left, SECTOR, 1), shifted(hop_right, SECTOR, 1)
    numbers = jnp.stack([block_dims[0], links[0, 0], place, core]).astype(jnp.int32)

    fixed = lambda rank: (lambda i, n: (0,) * rank)
    pack = pl.pallas_call(
        pack_kernel, out_shape=jax.ShapeDtypeStruct((PACK, LANES), i16), in_specs=[smem, vmem, vmem], out_specs=vmem,
        compiler_params=params, name="pack",
    )(numbers, v_left, v_right)

    def spread(rows):
        return lax.all_gather(rows, GROUP, axis=0, tiled=True)

    def across(own):
        pairs = [(i, i + 1) for i in range(1, count - 1, 2)]
        return lax.ppermute(own, SECTOR, pairs + [(b, a) for a, b in pairs])

    packs = spread(pack[None])

    def source(own):
        shapes = (jax.ShapeDtypeStruct((N, N), f32),) + ((message_shape,) if own else ())
        which = (lambda n: n[3]) if own else (lambda n: 1 - n[3])
        return pl.pallas_call(
            lambda *refs: source_kernel(*refs, own=own), out_shape=shapes,
            grid_spec=pltpu.PrefetchScalarGridSpec(
                num_scalar_prefetch=1, grid=(PEERS // 2,),
                in_specs=[block((1, PACK, LANES), lambda t, n: (2 * t + which(n), 0, 0)), block(everyone.shape, fixed(3))],
                out_specs=tuple(block(shape.shape, fixed(len(shape.shape))) for shape in shapes),
                scratch_shapes=[pltpu.VMEM((N, PEERS // 2 * LANES), bf16)] * 2 + [pltpu.VMEM((PEERS // 2 * LANES, N), bf16)],
            ),
            compiler_params=params, name="source",
        )(numbers, packs, everyone)

    def summed(messages, fields, norm=None):
        specs = [block((1, ROWS, N), lambda i, n, c=c: (1 + c - n[3], n[2], 0)) for c in (0, 1)]
        shapes = (spread_shape,) + (() if norm is None else (jax.ShapeDtypeStruct((count, 8, LANES), f32),))
        more = () if norm is None else (norm,)
        return pl.pallas_call(
            sum_kernel, out_shape=shapes,
            grid_spec=pltpu.PrefetchScalarGridSpec(
                num_scalar_prefetch=1, grid=(1,),
                in_specs=[block((PEERS, MESSAGE, LANES), fixed(3))] + specs + [block((8, LANES), fixed(2))] * len(more),
                out_specs=tuple(block(shape.shape, fixed(3)) for shape in shapes),
            ),
            compiler_params=params, name="sum",
        )(numbers, messages, fields, fields, *more)

    def dots(messages, fields):
        return pl.pallas_call(
            dots_kernel, out_shape=(jax.ShapeDtypeStruct((count, 8, LANES), f32), message_shape),
            grid_spec=pltpu.PrefetchScalarGridSpec(
                num_scalar_prefetch=1, grid=(1,),
                in_specs=[block((2 * PEERS, MESSAGE, LANES), fixed(3)), block((1, N, N), lambda i, n: (1, 0, 0))],
                out_specs=(block((count, 8, LANES), fixed(3)), block((PEERS, MESSAGE, LANES), fixed(3))),
            ),
            compiler_params=params, name="dots",
        )(numbers, messages, fields)

    def applied(step, messages, far, extra):
        shapes = (field3, message_shape) + (small,) * step
        return pl.pallas_call(
            lambda *refs: apply_kernel(*refs, count=step), out_shape=shapes,
            in_specs=[smem] + [vmem] * (2 + len(extra) + 5), out_specs=(vmem,) * len(shapes),
            scratch_shapes=[pltpu.VMEM((3, 2, N, N), bf16), pltpu.VMEM((2, N, N), bf16), pltpu.VMEM((N, N), f32)],
            compiler_params=params, name="apply",
        )(numbers, messages, far, *extra, left, right, hop_in, hop_out, back)

    mine, own = source(True)
    far = across(own)
    back_out, mine = lax.optimization_barrier((back_out, mine))
    messages, extra = mine, tuple(source(False))
    pair = jax.ShapeDtypeStruct((2, N, N), bf16)
    four = jax.ShapeDtypeStruct((4, N, N), bf16)
    left, right, hop_in, hop_out, back = pl.pallas_call(
        split_kernel, out_shape=(pair, pair, pair, pair, four), in_specs=[vmem] * 6, out_specs=(vmem,) * 5,
        compiler_params=params, name="split",
    )(left_ops, right_ops, hop_left, hop_right, back_in, back_out)
    fields, past = [], None
    for step in range(3):
        if step:
            partial, own = dots(messages, fields[-1])
            far = across(own)
            totals = lax.all_to_all(partial, SECTOR, 0, 0, tiled=True)
            extra = (fields[-1], totals) + (() if step == 1 else (fields[-2], past))
        now, rows, *tail = applied(step, messages, far, extra)
        fields.append(now)
        past = tail[0] if tail else None
        rows, *sums = summed(exchange(rows), now, tail[1] if step == 2 else None)
        if step == 2:
            totals = lax.all_to_all(sums[0], SECTOR, 0, 0, tiled=True)
        messages = spread(rows)
    tall = block((1, N // PARTS, N), lambda i, n: (1, i, 0))
    flat = block((1, N // PARTS, N), lambda i, n: (0, i, 0))
    return tuple(
        pl.pallas_call(
            last_kernel, out_shape=(whole, whole),
            grid_spec=pltpu.PrefetchScalarGridSpec(
                num_scalar_prefetch=1, grid=(PARTS,),
                in_specs=[block((2 * PEERS // PARTS, MESSAGE, LANES), lambda i, n: (i, 0, 0))] + [tall] * 3
                + [block((count, 8, LANES), fixed(3)), block((8, LANES), fixed(2))],
                out_specs=(flat, flat),
            ),
            compiler_params=params, name="last",
        )(numbers, messages, stay(fields[0]), stay(fields[1]), stay(fields[2]), totals, past)
    )


def solution(mesh):
    finer = Mesh(mesh.devices.reshape(mesh.shape["term"], 4, 4, 2), ("term", "sector_0", "sector_1", "core"))
    both = P("term", SECTOR, None, None)
    in_specs = (both,) * 6 + (P(SECTOR, None, None), P("term", SECTOR), P(SECTOR))
    out_specs = (P(SECTOR, None, None), P(SECTOR, None, None))
    return jax.shard_map(body, mesh=finer, in_specs=in_specs, out_specs=out_specs, check_vma=False)
```
